32 devices in a mesh: ctx: 16 (over z, y, core), head: 2 (over x).
Axes of the slice: x: 2, y: 2, z: 4, core: 2. Of those that a mesh axis runs over, the one named last changes fastest.
Arguments:
- queries: bfloat16 [4096, 4096], P(('ctx', 'head')), may hold values from -6 to 6
- keys: bfloat16 [4096, 1024], P(('ctx', 'head')), may hold values from -6 to 6
- values: bfloat16 [4096, 1024], P(('ctx', 'head')), may hold values from -6 to 6
- grad_out: bfloat16 [4096, 4096], P(('ctx', 'head')), may hold values from -6 to 6
- doc_ids: int32 [4096], replicated, may hold values from 0 to 3, never falling along the last dimension, each value on 1 to 2048 neighbouring positions
Outputs:
- attended: bfloat16 [4096, 4096], P(('ctx', 'head'))
- grad_queries: bfloat16 [4096, 4096], P(('ctx', 'head'))
- grad_keys: bfloat16 [4096, 1024], P(('ctx', 'head'))
- grad_values: bfloat16 [4096, 1024], P(('ctx', 'head'))
The draws below stay inside these ranges and needn't reach their ends.
Inputs may be any that keep to these rules, and one draw needn't show every extreme that they name: `doc_ids`: document numbers never fall along the row; every document has 1 to 2048 tokens and one has exactly 2048.
All inputs are finite; a program needn't handle non-finite values.
Results may differ from the reference program's by a relative error of at most 0.023.
Values may be sent and summed in bfloat16 or wider, within the bound.
A program may use at most 64 MiB of HBM per device.

```python
import math
import jax
import jax.numpy as jnp
import numpy as np
from jax import lax

QH = 32
KVH = 8
HD = 128
TOK_DEV = 256
DOC_MOST = 2048
TOKENS = 4096
DOCS = 4
DOC_LONG = 2048


def draw_queries(key, part):
    drawn = jnp.clip(jax.random.normal(jax.random.fold_in(key, 11), (TOKENS, QH * HD), jnp.float32), -6.0, 6.0)
    return drawn.astype(jnp.bfloat16)


def draw_keys(key, part):
    drawn = jnp.clip(jax.random.normal(jax.random.fold_in(key, 12), (TOKENS, KVH * HD), jnp.float32), -6.0, 6.0)
    return drawn.astype(jnp.bfloat16)


def steps_of(rng, extent, shards, low, largest):
    def one(dim, shards_of):
        draws = jax.random.uniform(jax.random.fold_in(jax.random.fold_in(rng, 6), dim), (shards_of,), jnp.float32, low / len(shards), largest / len(shards))
        return jnp.repeat(jnp.exp(draws), extent[dim] // shards_of).reshape((-1,) + (1,) * (len(extent) - dim - 1))

    factor_of = one(*shards[0])
    for cut in shards[1:]:
        factor_of = factor_of * one(*cut)
    return factor_of


def length_profile(number_of, total, limit, skew):
    portions = [(1 << 20) // math.isqrt(grade ** skew) + 1 for grade in range(2, number_of + 1)]
    rest, given = total - limit - (number_of - 1), [1] * (number_of - 1)
    while rest > 0:
        candidates = [i for i in range(number_of - 1) if given[i] < limit]
        pool, left = sum([portions[i] for i in candidates]), rest
        for i in candidates:
            addition = min(limit - given[i], max(1, left * portions[i] // pool), rest)
            given[i] = given[i] + addition
            rest = rest - addition
    return np.array([limit] + given)


def ragged_sizes(key, amount, total, limit, slope):
    if amount == 2:
        one = jax.random.randint(key, (), max(1, total - limit), min(limit, total - 1) + 1)
        return jnp.stack([one, total - one])
    tallies = jnp.asarray(length_profile(amount, total, limit, slope), jnp.int32)
    pairs = (amount - 1) // 2
    donor, taker = tallies[1:1 + 2 * pairs:2], tallies[2:2 + 2 * pairs:2]
    slack = jnp.minimum(donor - 1, limit - taker)
    passed = jax.random.randint(jax.random.fold_in(key, 1), (pairs,), 0, 1 << 20) % (slack + 1)
    tallies = tallies.at[1:1 + 2 * pairs:2].set(donor - passed).at[2:2 + 2 * pairs:2].set(taker + passed)
    return tallies[jax.random.permutation(jax.random.fold_in(key, 2), amount)]


def centred(key, shape, width, most, cuts=(), kind=jnp.bfloat16):
    entries = width * jax.random.normal(key, shape, jnp.float32)
    if cuts:
        entries = entries * steps_of(key, shape, cuts, -0.22, 0.18)
    return jnp.clip(entries, -most, most).astype(kind)


def setup_inputs(seed: int = 0) -> dict:
    key_of = jax.random.split(jax.random.key(seed), 6)
    queries = draw_queries(jax.random.fold_in(key_of[5], 71), 0)
    keys = draw_keys(jax.random.fold_in(key_of[5], 71), 0)
    values = centred(key_of[2], (TOKENS, KVH * HD), 1.0, 6.0, ((0, 32),))
    grad_out = centred(key_of[3], (TOKENS, QH * HD), 1.0, 6.0, ((0, 32),))
    doc_ids = jnp.searchsorted(jnp.cumsum(ragged_sizes(key_of[4], DOCS, TOKENS, DOC_LONG, 1)), jnp.arange(TOKENS), side="right").astype(jnp.int32)
    return {"queries": queries, "keys": keys, "values": values, "grad_out": grad_out, "doc_ids": doc_ids}


def reference(queries, keys, values, grad_out, doc_ids):
    softmax_scale = HD ** -0.5
    group_size = QH // KVH
    window = TOK_DEV + DOC_MOST
    padding = jnp.zeros((DOC_MOST, KVH * HD), jnp.bfloat16)
    key_pad = jnp.concatenate((padding, keys), 0)
    value_pad = jnp.concatenate((padding, values), 0)
    docs_all = doc_ids.astype(jnp.int32)
    doc_pad = jnp.concatenate((jnp.full((DOC_MOST,), -1, jnp.int32), docs_all), 0)
    offsets = jnp.arange(window, dtype=jnp.int32)
    row_ids = jnp.arange(TOK_DEV, dtype=jnp.int32)

    def block_step(carried, block_index):
        grad_key_all, grad_value_all = carried
        row_start = (block_index * TOK_DEV).astype(jnp.int32)
        query_blk = lax.dynamic_slice_in_dim(queries, row_start, TOK_DEV, 0).astype(jnp.float32).reshape(TOK_DEV, KVH, group_size, HD)
        grad_blk = lax.dynamic_slice_in_dim(grad_out, row_start, TOK_DEV, 0).astype(jnp.float32).reshape(TOK_DEV, KVH, group_size, HD)
        key_blk = lax.dynamic_slice_in_dim(key_pad, row_start, window, 0).astype(jnp.float32).reshape(window, KVH, HD)
        value_blk = lax.dynamic_slice_in_dim(value_pad, row_start, window, 0).astype(jnp.float32).reshape(window, KVH, HD)
        doc_keys = lax.dynamic_slice_in_dim(doc_pad, row_start, window, 0)
        doc_rows = lax.dynamic_slice_in_dim(docs_all, row_start, TOK_DEV, 0)
        visible = (doc_rows[:, None] == doc_keys[None, :]) & (offsets[None, :] <= row_ids[:, None] + DOC_MOST)
        scores = jnp.einsum("tkgd,wkd->kgtw", query_blk, key_blk) * softmax_scale
        scores = jnp.where(visible, scores, -1e30)
        row_peak = jnp.max(scores, -1, keepdims=True)
        exponent = jnp.where(visible, jnp.exp(scores - row_peak), 0.0)
        row_total = jnp.sum(exponent, -1, keepdims=True)
        weights_low = (exponent / row_total).astype(jnp.bfloat16)
        weights = lax.optimization_barrier(weights_low).astype(jnp.float32)
        attended = jnp.einsum("kgtw,wkd->tkgd", weights, value_blk).astype(jnp.bfloat16)
        grad_weights = jnp.einsum("tkgd,wkd->kgtw", grad_blk, value_blk)
        row_delta = jnp.sum(weights * grad_weights, -1, keepdims=True)
        scores_low = (weights * (grad_weights - row_delta)).astype(jnp.bfloat16)
        grad_scores = lax.optimization_barrier(scores_low).astype(jnp.float32)
        grad_query = (jnp.einsum("kgtw,wkd->tkgd", grad_scores, key_blk) * softmax_scale).astype(jnp.bfloat16)
        key_term = (jnp.einsum("kgtw,tkgd->wkd", grad_scores, query_blk) * softmax_scale).reshape(window, KVH * HD)
        value_term = jnp.einsum("kgtw,tkgd->wkd", weights, grad_blk).reshape(window, KVH * HD)
        grad_key_all = lax.dynamic_update_slice_in_dim(grad_key_all, lax.dynamic_slice_in_dim(grad_key_all, row_start, window, 0) + key_term, row_start, 0)
        grad_value_all = lax.dynamic_update_slice_in_dim(grad_value_all, lax.dynamic_slice_in_dim(grad_value_all, row_start, window, 0) + value_term, row_start, 0)
        return (grad_key_all, grad_value_all), (attended.reshape(TOK_DEV, QH * HD), grad_query.reshape(TOK_DEV, QH * HD))

    initial = (jnp.zeros((TOKENS + DOC_MOST, KVH * HD), jnp.float32), jnp.zeros((TOKENS + DOC_MOST, KVH * HD), jnp.float32))
    sums, outputs = lax.scan(block_step, initial, jnp.arange(TOKENS // TOK_DEV, dtype=jnp.int32))
    attended_all = outputs[0].reshape(TOKENS, QH * HD)
    grad_query_all = outputs[1].reshape(TOKENS, QH * HD)
    return attended_all, grad_query_all, sums[0][DOC_MOST:].astype(jnp.bfloat16), sums[1][DOC_MOST:].astype(jnp.bfloat16)
```

```python
import functools

import jax
import jax.numpy as jnp
from jax import lax
from jax.experimental import pallas as pl
from jax.experimental.pallas import tpu as pltpu
from jax.sharding import PartitionSpec as P

HD = 128
DOC_MOST = 2048
TILE = 256
LOG2E = 1.4426950408889634
MESH = pl.DeviceIdType.MESH


def place(ctx_low, heads):
    ctx, head = lax.axis_index("ctx"), lax.axis_index("head")
    block = ctx // ctx_low
    me = (ctx - block * ctx_low) * heads + head

    def member(number):
        return (block * ctx_low + number // heads, lax.rem(number, heads))

    return ctx, head, block, me, member


def greet(members, ctx, head, ctx_low, has_prev, has_next):
    barrier = pltpu.get_barrier_semaphore()
    for device in members:
        pl.semaphore_signal(barrier, inc=1, device_id=device, device_id_type=MESH)

    @pl.when(has_prev)
    def _():
        pl.semaphore_signal(barrier, inc=1, device_id=(ctx - ctx_low, head), device_id_type=MESH)

    @pl.when(has_next)
    def _():
        pl.semaphore_signal(barrier, inc=1, device_id=(ctx + ctx_low, head), device_id_type=MESH)

    near = has_prev.astype(jnp.int32) + has_next.astype(jnp.int32)
    pl.semaphore_wait(barrier, len(members) + near)


def fused_kernel(
    heads, ctx_low, blocks, distance, scale,
    doc_ref, q_in, k_in, v_in, g_in,
    ao_ref, do_ref, ko_ref, vo_ref,
    qo, go, band, acc, kept, peak, total, ot, dqt, kt, vt, inv, delta,
    att, dq, sums, landed, wide, seen_doc,
    own_sem, send_sem, recv_sem, in_send, in_recv, out_send, out_recv,
):
    group = ctx_low * heads
    rows = q_in.shape[0]
    q_cols = q_in.shape[1] // group
    tokens = qo.shape[0] * TILE
    share = q_cols // HD
    factor = scale * LOG2E
    per_block = tokens // TILE
    per_tile = TILE // rows
    reach = distance * per_block + 1
    ctx, head, block, me, member = place(ctx_low, heads)
    has_prev, has_next = block > 0, block < blocks - 1
    others = [lax.rem(me + step, group) for step in range(1, group)]
    greet([member(o) for o in others], ctx, head, ctx_low, has_prev, has_next)
    my_tile = me // per_tile
    my_row = (me - my_tile * per_tile) * rows
    mine = pl.ds(pl.multiple_of(me * rows, rows), rows)
    first_tile = (block - distance) * per_block
    first_kb = jnp.maximum(distance - block, 0) * per_block

    def columns(width, number):
        return pl.ds(pl.multiple_of(number * width, width), width)

    def swap_in(a, src, first, width, dst):
        def part(number):
            return src.at[:, pl.ds(pl.multiple_of(number * width + first, HD), HD)]

        local = pltpu.make_async_copy(part(me), dst, own_sem.at[a])
        local.start()
        line = []
        for step, other in enumerate(others):
            copy = pltpu.make_async_remote_copy(
                src_ref=part(other), dst_ref=dst,
                send_sem=send_sem.at[a, step], recv_sem=recv_sem.at[a, step],
                device_id=member(other), device_id_type=MESH,
            )
            copy.start()
            line.append(copy)
        return local, line

    def head_rows(h):
        return pl.ds(pl.multiple_of(h * TILE + my_row, rows), rows)

    def settle(pair):
        pair[0].wait()
        for copy in pair[1]:
            copy.wait_recv()

    def tile_out(a, i, src, width, dst):
        def one(j, _):
            number = i * per_tile + j
            step = lax.rem(number - me + group, group)
            piece = src.at[pl.ds(pl.multiple_of(number * rows, rows), rows)]
            place_there = dst.at[:, columns(width, me)]

            @pl.when(step == 0)
            def _():
                pltpu.make_async_copy(piece, place_there, own_sem.at[a]).start()

            @pl.when(step > 0)
            def _():
                pltpu.make_async_remote_copy(
                    src_ref=piece, dst_ref=place_there,
                    send_sem=send_sem.at[a, step - 1], recv_sem=recv_sem.at[a, step - 1],
                    device_id=member(number), device_id_type=MESH,
                ).start()

            return 0

        lax.fori_loop(0, per_tile, one, 0)

    def end_out(a, src, width, dst):
        piece, place_there = src.at[mine], dst.at[:, columns(width, me)]
        pltpu.make_async_copy(piece, place_there, own_sem.at[a]).wait()
        for step, other in enumerate(others):
            copy = pltpu.make_async_remote_copy(
                src_ref=src.at[pl.ds(pl.multiple_of(other * rows, rows), rows)],
                dst_ref=place_there,
                send_sem=send_sem.at[a, step], recv_sem=recv_sem.at[a, step],
                device_id=member(other), device_id_type=MESH,
            )
            copy.wait_recv()
            copy.wait_send()

    def hop_in(step, c):
        return pltpu.make_async_remote_copy(
            src_ref=band.at[distance - step, c], dst_ref=band.at[distance - step - 1, c],
            send_sem=in_send.at[step, c], recv_sem=in_recv.at[step, c],
            device_id=(ctx + ctx_low, head), device_id_type=MESH,
        )

    def hop_out(step, c, t):
        return pltpu.make_async_remote_copy(
            src_ref=sums.at[step, c, tile_rows(t)], dst_ref=landed.at[step, c, tile_rows(t)],
            send_sem=out_send.at[step, c, t], recv_sem=out_recv.at[step, c, t],
            device_id=(ctx - ctx_low, head), device_id_type=MESH,
        )

    def tile_rows(i):
        return pl.ds(pl.multiple_of(i * TILE, TILE), TILE)

    kv_swap = [
        swap_in(0, k_in, 0, HD, band.at[distance, 0, mine]),
        swap_in(1, v_in, 0, HD, band.at[distance, 1, mine]),
    ]
    q_swap = [
        swap_in(2 + h, q_in, h * HD, q_cols, qo.at[my_tile, head_rows(h)]) for h in range(share)
    ]
    g_swap = [
        swap_in(2 + share + h, g_in, h * HD, q_cols, go.at[my_tile, head_rows(h)])
        for h in range(share)
    ]
    out_at = 2 + 2 * share
    acc[...] = jnp.zeros_like(acc)
    dqt[...] = jnp.zeros_like(dqt)
    peak[...] = jnp.full_like(peak, -1e30)
    for c in range(2):
        settle(kv_swap[c])

        @pl.when(has_next)
        def _():
            hop_in(0, c).start()

    for step in range(1, distance):
        @pl.when(block - step >= 0)
        def _():
            for c in range(2):
                hop_in(step - 1, c).wait_recv()

                @pl.when(has_next)
                def _():
                    hop_in(step, c).start()

    for pair in q_swap:
        settle(pair)

    spans = [slice(h * TILE, (h + 1) * TILE) for h in range(share)]
    cols = [slice(h * HD, (h + 1) * HD) for h in range(share)]

    def across(x, y):
        return lax.dot_general(
            x, y, (((1,), (1,)), ((), ())), preferred_element_type=jnp.float32
        )

    def fold(x, op):
        return op(x.reshape(TILE // 8, 8, TILE), 0)

    def score_slot(n, _):
        slot = distance - n

        @pl.when(block - n >= 0)
        def _():
            @pl.when(n == distance)
            def _():
                for c in range(2):
                    hop_in(distance - 1, c).wait_recv()

            def key_step(t, _):
                kb = slot * per_block + t
                here = tile_rows(t)
                keys = band[slot, 0, here, :]
                kt[kb] = keys.T
                vt[kb] = band[slot, 1, here, :].T
                docs = jnp.broadcast_to(doc_ref[first_tile + kb], (HD, TILE))
                seen_doc[...] = docs.T

                def row_step(i, _):
                    away = lax.broadcasted_iota(jnp.int32, (TILE, TILE), 1) - (
                        lax.broadcasted_iota(jnp.int32, (TILE, TILE), 0)
                    )
                    theirs = seen_doc[...]
                    same = jnp.concatenate([theirs, theirs], 1) == doc_ref[block * per_block + i]
                    seen = same & (away >= (kb - i - reach + 1) * TILE)
                    for h in range(share):
                        s = across(keys, qo[i, spans[h], :])
                        s = jnp.where(seen, s, -1e30)
                        kept[i, kb - i, :, spans[h]] = s
                        peak[i, :, spans[h]] = jnp.maximum(peak[i, :, spans[h]], fold(s, jnp.max))
                    return 0

                lax.fori_loop(
                    jnp.maximum(kb - reach + 1, 0), jnp.minimum(kb + 1, per_block), row_step, 0
                )
                return 0

            lax.fori_loop(0, per_block, key_step, 0)

        return 0

    lax.fori_loop(0, distance + 1, score_slot, 0)
    for pair in g_swap:
        settle(pair)

    def forward_tile(i, _):
        here = tile_rows(i)
        top = jnp.max(peak[i], 0, keepdims=True) * factor
        total[...] = jnp.zeros_like(total)
        ot[...] = jnp.zeros_like(ot)

        def forward(kb, _):
            values_t = vt[kb]
            for h in range(share):
                span = spans[h]
                p = jnp.exp2(kept[i, kb - i, :, span] * factor - top[:, span])
                kept[i, kb - i, :, span] = p
                total[:, span] += fold(p, jnp.sum)
                ot[:, span] += jnp.dot(
                    values_t, p.astype(jnp.bfloat16), preferred_element_type=jnp.float32
                )
            return 0

        lax.fori_loop(jnp.maximum(i, first_kb), i + reach, forward, 0)
        inverse = 1.0 / jnp.sum(total[...], 0, keepdims=True)
        inv[i] = inverse
        for h in range(share):
            out = ot[:, spans[h]] * inverse[:, spans[h]]
            grads = go[i, spans[h], :].T.astype(jnp.float32)
            delta[i, :, spans[h]] = jnp.sum(out * grads, 0, keepdims=True)
            att[here, cols[h]] = out.T.astype(jnp.bfloat16)
        tile_out(out_at, i, att, q_cols, ao_ref)
        return 0

    lax.fori_loop(0, per_block, forward_tile, 0)

    def back_slot(slot, _):
        @pl.when(block - (distance - slot) >= 0)
        def _():
            def key_step(t, _):
                kb = slot * per_block + t
                values = band[slot, 1, tile_rows(t), :]
                keys_t = kt[kb]

                def row_step(i, _):
                    inverse, shift = inv[i], delta[i]
                    for h in range(share):
                        span = spans[h]
                        w = kept[i, kb - i, :, span] * inverse[:, span]
                        dp = across(values, go[i, span, :])
                        wide[0, :, span] = w.astype(jnp.bfloat16)
                        wide[1, :, span] = (w * (dp - shift[:, span])).astype(jnp.bfloat16)
                    dqt[i] += jnp.dot(keys_t, wide[1], preferred_element_type=jnp.float32)
                    acc[0, kb] += jnp.dot(wide[1], qo[i], preferred_element_type=jnp.float32)
                    acc[1, kb] += jnp.dot(wide[0], go[i], preferred_element_type=jnp.float32)
                    return 0

                lax.fori_loop(
                    jnp.maximum(kb - reach + 1, 0), jnp.minimum(kb + 1, per_block), row_step, 0
                )

                @pl.when(slot < distance)
                def _():
                    send_term(slot, t)

                @pl.when(slot == distance)
                def _():
                    for h in range(share):
                        dq[tile_rows(t), cols[h]] = (
                            (dqt[t, :, spans[h]] * scale).T.astype(jnp.bfloat16)
                        )
                    tile_out(out_at + 1, t, dq, q_cols, do_ref)

                return 0

            lax.fori_loop(0, per_block, key_step, 0)

        return 0

    def close_term(slot, c, t):
        by = scale if c == 0 else 1.0
        term = acc[c, slot * per_block + t] * by

        @pl.when((slot > 0) & has_next)
        def _():
            hop_out(slot - 1, c, t).wait_recv()
            both = term + landed[slot - 1, c, tile_rows(t), :].astype(jnp.float32)
            sums[slot, c, tile_rows(t), :] = both.astype(jnp.bfloat16)

        @pl.when(jnp.logical_not((slot > 0) & has_next))
        def _():
            sums[slot, c, tile_rows(t), :] = term.astype(jnp.bfloat16)

    def send_term(slot, t):
        for c in range(2):
            close_term(slot, c, t)
        for c in range(2):
            hop_out(slot, c, t).start()

    lax.fori_loop(0, distance + 1, back_slot, 0)

    def finish(t, _):
        for c in range(2):
            close_term(distance, c, t)
        tile_out(out_at + 2, t, sums.at[distance, 0], HD, ko_ref)
        tile_out(out_at + 3, t, sums.at[distance, 1], HD, vo_ref)
        return 0

    lax.fori_loop(0, per_block, finish, 0)
    for pair in kv_swap + q_swap + g_swap:
        for copy in pair[1]:
            copy.wait_send()
    end_out(out_at, att, q_cols, ao_ref)
    end_out(out_at + 1, dq, q_cols, do_ref)
    end_out(out_at + 2, sums.at[distance, 0], HD, ko_ref)
    end_out(out_at + 3, sums.at[distance, 1], HD, vo_ref)
    for c in range(2):
        for step in range(distance):
            @pl.when((block - step >= 0) & has_next)
            def _():
                hop_in(step, c).wait_send()

            @pl.when(block - (distance - step) >= 0)
            def _():
                for t in range(per_block):
                    hop_out(step, c, t).wait_send()


def per_device(queries, keys, values, grad_out, doc_ids):
    heads = lax.axis_size("head")
    peers = lax.axis_size("ctx")
    rows = queries.shape[0]
    group = keys.shape[1] // HD
    share = queries.shape[1] // HD // group
    ctx_low = group // heads
    blocks = peers // ctx_low
    tokens = rows * group
    distance = DOC_MOST // tokens
    bf16, f32 = jnp.bfloat16, jnp.float32
    vmem = pl.BlockSpec(memory_space=pltpu.VMEM)
    hbm = pl.BlockSpec(memory_space=pl.ANY)
    dma = pltpu.SemaphoreType.DMA
    tiles = tokens // TILE
    span = share * TILE
    all_tiles = (distance + 1) * tiles
    swaps = 2 + 2 * share + 4
    return pl.pallas_call(
        functools.partial(fused_kernel, heads, ctx_low, blocks, distance, HD ** -0.5),
        out_shape=(
            jax.ShapeDtypeStruct(queries.shape, bf16),
            jax.ShapeDtypeStruct(queries.shape, bf16),
            jax.ShapeDtypeStruct(keys.shape, bf16),
            jax.ShapeDtypeStruct(keys.shape, bf16),
        ),
        in_specs=[vmem] + [hbm] * 4,
        out_specs=(hbm,) * 4,
        scratch_shapes=[
            pltpu.VMEM((tiles, span, HD), bf16),
            pltpu.VMEM((tiles, span, HD), bf16),
            pltpu.VMEM((distance + 1, 2, tokens, HD), bf16),
            pltpu.VMEM((2, all_tiles, TILE, HD), f32),
            pltpu.VMEM((tiles, distance * tiles + 1, TILE, span), f32),
            pltpu.VMEM((tiles, 8, span), f32),
            pltpu.VMEM((8, span), f32),
            pltpu.VMEM((HD, span), f32),
            pltpu.VMEM((tiles, HD, span), f32),
            pltpu.VMEM((all_tiles, HD, TILE), bf16),
            pltpu.VMEM((all_tiles, HD, TILE), bf16),
            pltpu.VMEM((tiles, 1, span), f32),
            pltpu.VMEM((tiles, 1, span), f32),
            pltpu.VMEM((tokens, share * HD), bf16),
            pltpu.VMEM((tokens, share * HD), bf16),
            pltpu.VMEM((distance + 1, 2, tokens, HD), bf16),
            pltpu.VMEM((distance, 2, tokens, HD), bf16),
            pltpu.VMEM((2, TILE, span), bf16),
            pltpu.VMEM((TILE, HD), jnp.int32),
            dma((swaps,)), dma((swaps, group - 1)), dma((swaps, group - 1)),
            dma((distance, 2)), dma((distance, 2)),
            dma((distance, 2, tiles)), dma((distance, 2, tiles)),
        ],
        compiler_params=pltpu.CompilerParams(
            collective_id=1, has_side_effects=True, vmem_limit_bytes=67043328
        ),
        name="fused",
    )(doc_ids.reshape(-1, 1, TILE), queries, keys, values, grad_out)


def solution(mesh):
    spec = P(("ctx", "head"), None)
    return jax.shard_map(
        per_device,
        mesh=mesh,
        in_specs=(spec, spec, spec, spec, P()),
        out_specs=(spec, spec, spec, spec),
        check_vma=False,
    )
```

```python
import functools

import jax
import jax.numpy as jnp
from jax import lax
from jax.experimental import pallas as pl
from jax.experimental.pallas import tpu as pltpu
from jax.sharding import PartitionSpec as P

HD = 128
DOC_MOST = 2048
TILE = 256
LOG2E = 1.4426950408889634
MESH = pl.DeviceIdType.MESH


def place(ctx_low, heads):
    ctx, head = lax.axis_index("ctx"), lax.axis_index("head")
    block = ctx // ctx_low
    me = (ctx - block * ctx_low) * heads + head

    def member(number):
        return (block * ctx_low + number // heads, lax.rem(number, heads))

    return ctx, head, block, me, member


def greet(members, ctx, head, ctx_low, has_prev, has_next):
    barrier = pltpu.get_barrier_semaphore()
    for device in members:
        pl.semaphore_signal(barrier, inc=1, device_id=device, device_id_type=MESH)

    @pl.when(has_prev)
    def _():
        pl.semaphore_signal(barrier, inc=1, device_id=(ctx - ctx_low, head), device_id_type=MESH)

    @pl.when(has_next)
    def _():
        pl.semaphore_signal(barrier, inc=1, device_id=(ctx + ctx_low, head), device_id_type=MESH)

    near = has_prev.astype(jnp.int32) + has_next.astype(jnp.int32)
    pl.semaphore_wait(barrier, len(members) + near)


def fused_kernel(
    heads, ctx_low, blocks, distance, scale,
    doc_ref, q_in, k_in, v_in, g_in,
    ao_ref, do_ref, ko_ref, vo_ref,
    qo, go, band, acc, kept, peak, total, made, dqs, qt, gt, inv, delta,
    att, dq, sums, landed, wide, row_doc,
    own_sem, send_sem, recv_sem, in_send, in_recv, out_send, out_recv,
):
    group = ctx_low * heads
    rows = q_in.shape[0]
    q_cols = q_in.shape[1] // group
    tokens = qo.shape[0] * TILE
    share = q_cols // HD
    factor = scale * LOG2E
    per_block = tokens // TILE
    per_tile = TILE // rows
    reach = distance * per_block + 1
    ctx, head, block, me, member = place(ctx_low, heads)
    has_prev, has_next = block > 0, block < blocks - 1
    others = [lax.rem(me + step, group) for step in range(1, group)]
    greet([member(o) for o in others], ctx, head, ctx_low, has_prev, has_next)
    my_tile = me // per_tile
    my_row = (me - my_tile * per_tile) * rows
    mine = pl.ds(pl.multiple_of(me * rows, rows), rows)
    first_tile = (block - distance) * per_block
    first_kb = jnp.maximum(distance - block, 0) * per_block

    def columns(width, number):
        return pl.ds(pl.multiple_of(number * width, width), width)

    def swap_in(a, src, first, width, dst):
        def part(number):
            return src.at[:, pl.ds(pl.multiple_of(number * width + first, HD), HD)]

        local = pltpu.make_async_copy(part(me), dst, own_sem.at[a])
        local.start()
        line = []
        for step, other in enumerate(others):
            copy = pltpu.make_async_remote_copy(
                src_ref=part(other), dst_ref=dst,
                send_sem=send_sem.at[a, step], recv_sem=recv_sem.at[a, step],
                device_id=member(other), device_id_type=MESH,
            )
            copy.start()
            line.append(copy)
        return local, line

    def head_rows(h):
        return pl.ds(pl.multiple_of(h * TILE + my_row, rows), rows)

    def settle(pair):
        pair[0].wait()
        for copy in pair[1]:
            copy.wait_recv()

    def tile_out(a, i, src, width, dst):
        def one(j, _):
            number = i * per_tile + j
            step = lax.rem(number - me + group, group)
            piece = src.at[pl.ds(pl.multiple_of(number * rows, rows), rows)]
            place_there = dst.at[:, columns(width, me)]

            @pl.when(step == 0)
            def _():
                pltpu.make_async_copy(piece, place_there, own_sem.at[a]).start()

            @pl.when(step > 0)
            def _():
                pltpu.make_async_remote_copy(
                    src_ref=piece, dst_ref=place_there,
                    send_sem=send_sem.at[a, step - 1], recv_sem=recv_sem.at[a, step - 1],
                    device_id=member(number), device_id_type=MESH,
                ).start()

            return 0

        lax.fori_loop(0, per_tile, one, 0)

    def end_out(a, src, width, dst):
        piece, place_there = src.at[mine], dst.at[:, columns(width, me)]
        pltpu.make_async_copy(piece, place_there, own_sem.at[a]).wait()
        for step, other in enumerate(others):
            copy = pltpu.make_async_remote_copy(
                src_ref=src.at[pl.ds(pl.multiple_of(other * rows, rows), rows)],
                dst_ref=place_there,
                send_sem=send_sem.at[a, step], recv_sem=recv_sem.at[a, step],
                device_id=member(other), device_id_type=MESH,
            )
            copy.wait_recv()
            copy.wait_send()

    def hop_in(step, c):
        return pltpu.make_async_remote_copy(
            src_ref=band.at[distance - step, c], dst_ref=band.at[distance - step - 1, c],
            send_sem=in_send.at[step, c], recv_sem=in_recv.at[step, c],
            device_id=(ctx + ctx_low, head), device_id_type=MESH,
        )

    def hop_out(step, c, t):
        return pltpu.make_async_remote_copy(
            src_ref=sums.at[step, c, tile_rows(t)], dst_ref=landed.at[step, c, tile_rows(t)],
            send_sem=out_send.at[step, c, t], recv_sem=out_recv.at[step, c, t],
            device_id=(ctx - ctx_low, head), device_id_type=MESH,
        )

    def tile_rows(i):
        return pl.ds(pl.multiple_of(i * TILE, TILE), TILE)

    kv_swap = [
        swap_in(0, k_in, 0, HD, band.at[distance, 0, mine]),
        swap_in(1, v_in, 0, HD, band.at[distance, 1, mine]),
    ]
    q_swap = [
        swap_in(2 + h, q_in, h * HD, q_cols, qo.at[my_tile, head_rows(h)]) for h in range(share)
    ]
    g_swap = [
        swap_in(2 + share + h, g_in, h * HD, q_cols, go.at[my_tile, head_rows(h)])
        for h in range(share)
    ]
    out_at = 2 + 2 * share
    acc[...] = jnp.zeros_like(acc)
    dqs[...] = jnp.zeros_like(dqs)
    peak[...] = jnp.full_like(peak, -1e30)
    for i in range(per_block):
        row_doc[i] = jnp.broadcast_to(doc_ref[block * per_block + i], (HD, TILE)).T
    for c in range(2):
        settle(kv_swap[c])

        @pl.when(has_next)
        def _():
            hop_in(0, c).start()

    for step in range(1, distance):
        @pl.when(block - step >= 0)
        def _():
            for c in range(2):
                hop_in(step - 1, c).wait_recv()

                @pl.when(has_next)
                def _():
                    hop_in(step, c).start()

    for pair in q_swap:
        settle(pair)

    spans = [slice(h * TILE, (h + 1) * TILE) for h in range(share)]
    cols = [slice(h * HD, (h + 1) * HD) for h in range(share)]

    def across(x, y):
        return lax.dot_general(
            x, y, (((1,), (1,)), ((), ())), preferred_element_type=jnp.float32
        )

    def twice(x):
        return jnp.concatenate([x, x], 1)

    def score_slot(n, _):
        slot = distance - n

        @pl.when(block - n >= 0)
        def _():
            @pl.when(n == distance)
            def _():
                for c in range(2):
                    hop_in(distance - 1, c).wait_recv()

            def key_step(t, _):
                kb = slot * per_block + t

                def row_step(i, _):
                    keys = band[slot, 0, tile_rows(t), :]
                    away = lax.broadcasted_iota(jnp.int32, (TILE, TILE), 0) - (
                        lax.broadcasted_iota(jnp.int32, (TILE, TILE), 1)
                    )
                    same = twice(row_doc[i]) == doc_ref[first_tile + kb]
                    seen = same & (away >= (kb - i - reach + 1) * TILE)
                    for h in range(share):
                        s = jnp.where(seen, across(qo[i, spans[h], :], keys), -1e30)
                        kept[i, kb - i, spans[h], :] = s
                        both = jnp.maximum(s[:, :HD], s[:, HD:])
                        peak[i, spans[h], :] = jnp.maximum(peak[i, spans[h], :], both)
                    return 0

                lax.fori_loop(
                    jnp.maximum(kb - reach + 1, 0), jnp.minimum(kb + 1, per_block), row_step, 0
                )
                return 0

            lax.fori_loop(0, per_block, key_step, 0)

        return 0

    lax.fori_loop(0, distance + 1, score_slot, 0)
    for pair in g_swap:
        settle(pair)

    def forward_tile(i, _):
        here = tile_rows(i)
        for h in range(share):
            top = jnp.max(peak[i, spans[h], :], 1, keepdims=True) * factor
            peak[i, spans[h], :] = jnp.broadcast_to(top, (TILE, HD))
        total[...] = jnp.zeros_like(total)
        made[...] = jnp.zeros_like(made)

        def forward(kb, _):
            slot = kb // per_block
            values = band[slot, 1, tile_rows(kb - slot * per_block), :]
            for h in range(share):
                span = spans[h]
                p = jnp.exp2(kept[i, kb - i, span, :] * factor - twice(peak[i, span, :]))
                kept[i, kb - i, span, :] = p
                total[span, :] += p[:, :HD] + p[:, HD:]
                made[span, :] += jnp.dot(
                    p.astype(jnp.bfloat16), values, preferred_element_type=jnp.float32
                )
            return 0

        lax.fori_loop(jnp.maximum(i, first_kb), i + reach, forward, 0)
        for h in range(share):
            span = spans[h]
            inverse = 1.0 / jnp.sum(total[span, :], 1, keepdims=True)
            inv[i, span, :] = jnp.broadcast_to(inverse, (TILE, HD))
            out = made[span, :] * inverse
            shift = jnp.sum(out * go[i, span, :].astype(jnp.float32), 1, keepdims=True)
            delta[i, span, :] = jnp.broadcast_to(shift, (TILE, HD))
            att[here, cols[h]] = out.astype(jnp.bfloat16)
            qt[i, :, span] = qo[i, span, :].T
            gt[i, :, span] = go[i, span, :].T
        tile_out(out_at, i, att, q_cols, ao_ref)
        return 0

    lax.fori_loop(0, per_block, forward_tile, 0)

    def back_slot(slot, _):
        @pl.when(block - (distance - slot) >= 0)
        def _():
            def key_step(t, _):
                kb = slot * per_block + t

                def row_step(i, _):
                    keys = band[slot, 0, tile_rows(t), :]
                    values = band[slot, 1, tile_rows(t), :]
                    for h in range(share):
                        span = spans[h]
                        w = kept[i, kb - i, span, :] * twice(inv[i, span, :])
                        dp = across(go[i, span, :], values)
                        wide[0, span, :] = w.astype(jnp.bfloat16)
                        wide[1, span, :] = (w * (dp - twice(delta[i, span, :]))).astype(jnp.bfloat16)
                    for h in range(share):
                        dqs[i, spans[h], :] += jnp.dot(
                            wide[1, spans[h], :], keys, preferred_element_type=jnp.float32
                        )
                    acc[0, kb] += jnp.dot(qt[i], wide[1], preferred_element_type=jnp.float32)
                    acc[1, kb] += jnp.dot(gt[i], wide[0], preferred_element_type=jnp.float32)
                    return 0

                lax.fori_loop(
                    jnp.maximum(kb - reach + 1, 0), jnp.minimum(kb + 1, per_block), row_step, 0
                )

                @pl.when(slot < distance)
                def _():
                    send_term(slot, t)

                @pl.when(slot == distance)
                def _():
                    for h in range(share):
                        dq[tile_rows(t), cols[h]] = (dqs[t, spans[h], :] * scale).astype(jnp.bfloat16)
                    tile_out(out_at + 1, t, dq, q_cols, do_ref)

                return 0

            lax.fori_loop(0, per_block, key_step, 0)

        return 0

    def close_term(slot, c, t):
        by = scale if c == 0 else 1.0
        term = (acc[c, slot * per_block + t] * by).T

        @pl.when((slot > 0) & has_next)
        def _():
            hop_out(slot - 1, c, t).wait_recv()
            both = term + landed[slot - 1, c, tile_rows(t), :].astype(jnp.float32)
            sums[slot, c, tile_rows(t), :] = both.astype(jnp.bfloat16)

        @pl.when(jnp.logical_not((slot > 0) & has_next))
        def _():
            sums[slot, c, tile_rows(t), :] = term.astype(jnp.bfloat16)

    def send_term(slot, t):
        for c in range(2):
            close_term(slot, c, t)
        for c in range(2):
            hop_out(slot, c, t).start()

    lax.fori_loop(0, distance + 1, back_slot, 0)

    def finish(t, _):
        for c in range(2):
            close_term(distance, c, t)
        tile_out(out_at + 2, t, sums.at[distance, 0], HD, ko_ref)
        tile_out(out_at + 3, t, sums.at[distance, 1], HD, vo_ref)
        return 0

    lax.fori_loop(0, per_block, finish, 0)
    for pair in kv_swap + q_swap + g_swap:
        for copy in pair[1]:
            copy.wait_send()
    end_out(out_at, att, q_cols, ao_ref)
    end_out(out_at + 1, dq, q_cols, do_ref)
    end_out(out_at + 2, sums.at[distance, 0], HD, ko_ref)
    end_out(out_at + 3, sums.at[distance, 1], HD, vo_ref)
    for c in range(2):
        for step in range(distance):
            @pl.when((block - step >= 0) & has_next)
            def _():
                hop_in(step, c).wait_send()

            @pl.when(block - (distance - step) >= 0)
            def _():
                for t in range(per_block):
                    hop_out(step, c, t).wait_send()


def per_device(queries, keys, values, grad_out, doc_ids):
    heads = lax.axis_size("head")
    peers = lax.axis_size("ctx")
    rows = queries.shape[0]
    group = keys.shape[1] // HD
    share = queries.shape[1] // HD // group
    ctx_low = group // heads
    blocks = peers // ctx_low
    tokens = rows * group
    distance = DOC_MOST // tokens
    bf16, f32 = jnp.bfloat16, jnp.float32
    vmem = pl.BlockSpec(memory_space=pltpu.VMEM)
    hbm = pl.BlockSpec(memory_space=pl.ANY)
    dma = pltpu.SemaphoreType.DMA
    tiles = tokens // TILE
    span = share * TILE
    all_tiles = (distance + 1) * tiles
    swaps = 2 + 2 * share + 4
    return pl.pallas_call(
        functools.partial(fused_kernel, heads, ctx_low, blocks, distance, HD ** -0.5),
        out_shape=(
            jax.ShapeDtypeStruct(queries.shape, bf16),
            jax.ShapeDtypeStruct(queries.shape, bf16),
            jax.ShapeDtypeStruct(keys.shape, bf16),
            jax.ShapeDtypeStruct(keys.shape, bf16),
        ),
        in_specs=[vmem] + [hbm] * 4,
        out_specs=(hbm,) * 4,
        scratch_shapes=[
            pltpu.VMEM((tiles, span, HD), bf16),
            pltpu.VMEM((tiles, span, HD), bf16),
            pltpu.VMEM((distance + 1, 2, tokens, HD), bf16),
            pltpu.VMEM((2, all_tiles, HD, TILE), f32),
            pltpu.VMEM((tiles, distance * tiles + 1, span, TILE), f32),
            pltpu.VMEM((tiles, span, HD), f32),
            pltpu.VMEM((span, HD), f32),
            pltpu.VMEM((span, HD), f32),
            pltpu.VMEM((tiles, span, HD), f32),
            pltpu.VMEM((tiles, HD, span), bf16),
            pltpu.VMEM((tiles, HD, span), bf16),
            pltpu.VMEM((tiles, span, HD), f32),
            pltpu.VMEM((tiles, span, HD), f32),
            pltpu.VMEM((tokens, share * HD), bf16),
            pltpu.VMEM((tokens, share * HD), bf16),
            pltpu.VMEM((distance + 1, 2, tokens, HD), bf16),
            pltpu.VMEM((distance, 2, tokens, HD), bf16),
            pltpu.VMEM((2, span, TILE), bf16),
            pltpu.VMEM((tiles, TILE, HD), jnp.int32),
            dma((swaps,)), dma((swaps, group - 1)), dma((swaps, group - 1)),
            dma((distance, 2)), dma((distance, 2)),
            dma((distance, 2, tiles)), dma((distance, 2, tiles)),
        ],
        compiler_params=pltpu.CompilerParams(
            collective_id=1, has_side_effects=True, vmem_limit_bytes=67043328
        ),
        name="fused",
    )(doc_ids.reshape(-1, 1, TILE), queries, keys, values, grad_out)


def solution(mesh):
    spec = P(("ctx", "head"), None)
    return jax.shard_map(
        per_device,
        mesh=mesh,
        in_specs=(spec, spec, spec, spec, P()),
        out_specs=(spec, spec, spec, spec),
        check_vma=False,
    )
```

```python
import functools

import jax
import jax.numpy as jnp
from jax import lax
from jax.experimental import pallas as pl
from jax.experimental.pallas import tpu as pltpu
from jax.sharding import PartitionSpec as P

HD = 128
DOC_MOST = 2048
TILE = 256
LOG2E = 1.4426950408889634
MESH = pl.DeviceIdType.MESH


def place(ctx_low, heads):
    ctx, head = lax.axis_index("ctx"), lax.axis_index("head")
    block = ctx // ctx_low
    me = (ctx - block * ctx_low) * heads + head

    def member(number):
        return (block * ctx_low + number // heads, lax.rem(number, heads))

    return ctx, head, block, me, member


def greet(members, ctx, head, ctx_low, has_prev, has_next):
    barrier = pltpu.get_barrier_semaphore()
    for device in members:
        pl.semaphore_signal(barrier, inc=1, device_id=device, device_id_type=MESH)

    @pl.when(has_prev)
    def _():
        pl.semaphore_signal(barrier, inc=1, device_id=(ctx - ctx_low, head), device_id_type=MESH)

    @pl.when(has_next)
    def _():
        pl.semaphore_signal(barrier, inc=1, device_id=(ctx + ctx_low, head), device_id_type=MESH)

    near = has_prev.astype(jnp.int32) + has_next.astype(jnp.int32)
    pl.semaphore_wait(barrier, len(members) + near)


def fused_kernel(
    heads, ctx_low, blocks, distance, scale,
    doc_ref, q_in, k_in, v_in, g_in,
    ao_ref, do_ref, ko_ref, vo_ref,
    qo, go, band, acc, kept, peak, total, made, dqs, qt, gt, inv, delta,
    att, dq, sums, landed, wide, row_doc,
    own_sem, send_sem, recv_sem, in_send, in_recv, out_send, out_recv,
):
    group = ctx_low * heads
    rows = q_in.shape[0]
    q_cols = q_in.shape[1] // group
    tokens = qo.shape[0] * TILE
    share = q_cols // HD
    factor = scale * LOG2E
    per_block = tokens // TILE
    per_tile = TILE // rows
    reach = distance * per_block + 1
    ctx, head, block, me, member = place(ctx_low, heads)
    has_prev, has_next = block > 0, block < blocks - 1
    others = [lax.rem(me + step, group) for step in range(1, group)]
    greet([member(o) for o in others], ctx, head, ctx_low, has_prev, has_next)
    my_tile = me // per_tile
    my_row = (me - my_tile * per_tile) * rows
    mine = pl.ds(pl.multiple_of(me * rows, rows), rows)
    first_tile = (block - distance) * per_block
    first_kb = jnp.maximum(distance - block, 0) * per_block

    def columns(width, number):
        return pl.ds(pl.multiple_of(number * width, width), width)

    def swap_in(a, src, first, width, dst):
        def part(number):
            return src.at[:, pl.ds(pl.multiple_of(number * width + first, HD), HD)]

        local = pltpu.make_async_copy(part(me), dst, own_sem.at[a])
        local.start()
        line = []
        for step, other in enumerate(others):
            copy = pltpu.make_async_remote_copy(
                src_ref=part(other), dst_ref=dst,
                send_sem=send_sem.at[a, step], recv_sem=recv_sem.at[a, step],
                device_id=member(other), device_id_type=MESH,
            )
            copy.start()
            line.append(copy)
        return local, line

    def head_rows(h):
        return pl.ds(pl.multiple_of(h * TILE + my_row, rows), rows)

    def settle(pair):
        pair[0].wait()
        for copy in pair[1]:
            copy.wait_recv()

    def tile_out(a, i, src, width, dst):
        def one(j, _):
            number = i * per_tile + j
            step = lax.rem(number - me + group, group)
            piece = src.at[pl.ds(pl.multiple_of(number * rows, rows), rows)]
            place_there = dst.at[:, columns(width, me)]

            @pl.when(step == 0)
            def _():
                pltpu.make_async_copy(piece, place_there, own_sem.at[a]).start()

            @pl.when(step > 0)
            def _():
                pltpu.make_async_remote_copy(
                    src_ref=piece, dst_ref=place_there,
                    send_sem=send_sem.at[a, step - 1], recv_sem=recv_sem.at[a, step - 1],
                    device_id=member(number), device_id_type=MESH,
                ).start()

            return 0

        lax.fori_loop(0, per_tile, one, 0)

    def end_out(a, src, width, dst):
        piece, place_there = src.at[mine], dst.at[:, columns(width, me)]
        pltpu.make_async_copy(piece, place_there, own_sem.at[a]).wait()
        for step, other in enumerate(others):
            copy = pltpu.make_async_remote_copy(
                src_ref=src.at[pl.ds(pl.multiple_of(other * rows, rows), rows)],
                dst_ref=place_there,
                send_sem=send_sem.at[a, step], recv_sem=recv_sem.at[a, step],
                device_id=member(other), device_id_type=MESH,
            )
            copy.wait_recv()
            copy.wait_send()

    def hop_in(step, c):
        return pltpu.make_async_remote_copy(
            src_ref=band.at[distance - step, c], dst_ref=band.at[distance - step - 1, c],
            send_sem=in_send.at[step, c], recv_sem=in_recv.at[step, c],
            device_id=(ctx + ctx_low, head), device_id_type=MESH,
        )

    def hop_out(step, c, t):
        return pltpu.make_async_remote_copy(
            src_ref=sums.at[step, c, tile_rows(t)], dst_ref=landed.at[step, c, tile_rows(t)],
            send_sem=out_send.at[step, c, t], recv_sem=out_recv.at[step, c, t],
            device_id=(ctx - ctx_low, head), device_id_type=MESH,
        )

    def tile_rows(i):
        return pl.ds(pl.multiple_of(i * TILE, TILE), TILE)

    kv_swap = [
        swap_in(0, k_in, 0, HD, band.at[distance, 0, mine]),
        swap_in(1, v_in, 0, HD, band.at[distance, 1, mine]),
    ]
    q_swap = [
        swap_in(2 + h, q_in, h * HD, q_cols, qo.at[my_tile, head_rows(h)]) for h in range(share)
    ]
    g_swap = [
        swap_in(2 + share + h, g_in, h * HD, q_cols, go.at[my_tile, head_rows(h)])
        for h in range(share)
    ]
    out_at = 2 + 2 * share
    acc[...] = jnp.zeros_like(acc)
    dqs[...] = jnp.zeros_like(dqs)
    peak[...] = jnp.full_like(peak, -1e30)
    for i in range(per_block):
        row_doc[i] = jnp.broadcast_to(doc_ref[block * per_block + i], (HD, TILE)).T
    for c in range(2):
        settle(kv_swap[c])

        @pl.when(has_next)
        def _():
            hop_in(0, c).start()

    for step in range(1, distance):
        @pl.when(block - step >= 0)
        def _():
            for c in range(2):
                hop_in(step - 1, c).wait_recv()

                @pl.when(has_next)
                def _():
                    hop_in(step, c).start()

    for pair in q_swap:
        settle(pair)

    spans = [slice(h * TILE, (h + 1) * TILE) for h in range(share)]
    cols = [slice(h * HD, (h + 1) * HD) for h in range(share)]

    def across(x, y):
        return lax.dot_general(
            x, y, (((1,), (1,)), ((), ())), preferred_element_type=jnp.float32
        )

    def twice(x):
        return jnp.concatenate([x, x], 1)

    def score_slot(n, _):
        slot = distance - n

        @pl.when(block - n >= 0)
        def _():
            @pl.when(n == distance)
            def _():
                hop_in(distance - 1, 0).wait_recv()

            def key_step(t, _):
                kb = slot * per_block + t

                def row_step(i, _):
                    keys = band[slot, 0, tile_rows(t), :]
                    away = lax.broadcasted_iota(jnp.int32, (TILE, TILE), 0) - (
                        lax.broadcasted_iota(jnp.int32, (TILE, TILE), 1)
                    )
                    same = twice(row_doc[i]) == doc_ref[first_tile + kb]
                    seen = same & (away >= (kb - i - reach + 1) * TILE)
                    for h in range(share):
                        s = jnp.where(seen, across(qo[i, spans[h], :], keys), -1e30)
                        kept[i, kb - i, spans[h], :] = s
                        both = jnp.maximum(s[:, :HD], s[:, HD:])
                        peak[i, spans[h], :] = jnp.maximum(peak[i, spans[h], :], both)
                    return 0

                lax.fori_loop(
                    jnp.maximum(kb - reach + 1, 0), jnp.minimum(kb + 1, per_block), row_step, 0
                )
                return 0

            lax.fori_loop(0, per_block, key_step, 0)

        return 0

    lax.fori_loop(0, distance + 1, score_slot, 0)

    @pl.when(block - distance >= 0)
    def _():
        hop_in(distance - 1, 1).wait_recv()

    def forward_tile(i, _):
        here = tile_rows(i)
        for h in range(share):
            top = jnp.max(peak[i, spans[h], :], 1, keepdims=True) * factor
            peak[i, spans[h], :] = jnp.broadcast_to(top, (TILE, HD))
        total[...] = jnp.zeros_like(total)
        made[...] = jnp.zeros_like(made)

        def forward(kb, _):
            slot = kb // per_block
            values = band[slot, 1, tile_rows(kb - slot * per_block), :]
            for h in range(share):
                span = spans[h]
                p = jnp.exp2(kept[i, kb - i, span, :] * factor - twice(peak[i, span, :]))
                kept[i, kb - i, span, :] = p
                total[span, :] += p[:, :HD] + p[:, HD:]
                made[span, :] += jnp.dot(
                    p.astype(jnp.bfloat16), values, preferred_element_type=jnp.float32
                )
            return 0

        lax.fori_loop(jnp.maximum(i, first_kb), i + reach, forward, 0)
        for h in range(share):
            span = spans[h]
            inverse = 1.0 / jnp.sum(total[span, :], 1, keepdims=True)
            inv[i, span, :] = jnp.broadcast_to(inverse, (TILE, HD))
            out = made[span, :] * inverse
            delta[i, span, :] = out
            att[here, cols[h]] = out.astype(jnp.bfloat16)
            qt[i, :, span] = qo[i, span, :].T
        tile_out(out_at, i, att, q_cols, ao_ref)
        return 0

    lax.fori_loop(0, per_block, forward_tile, 0)

    for pair in g_swap:
        settle(pair)

    def shift_tile(i, _):
        for h in range(share):
            span = spans[h]
            grads = go[i, span, :]
            shift = jnp.sum(delta[i, span, :] * grads.astype(jnp.float32), 1, keepdims=True)
            delta[i, span, :] = jnp.broadcast_to(shift, (TILE, HD))
            gt[i, :, span] = grads.T
        return 0

    lax.fori_loop(0, per_block, shift_tile, 0)

    def back_tile(slot, t, i):
        kb = slot * per_block + t
        keys = band[slot, 0, tile_rows(t), :]
        values = band[slot, 1, tile_rows(t), :]
        for h in range(share):
            span = spans[h]
            w = kept[i, kb - i, span, :] * twice(inv[i, span, :])
            dp = across(go[i, span, :], values)
            wide[0, span, :] = w.astype(jnp.bfloat16)
            wide[1, span, :] = (w * (dp - twice(delta[i, span, :]))).astype(jnp.bfloat16)
        for h in range(share):
            dqs[i, spans[h], :] += jnp.dot(
                wide[1, spans[h], :], keys, preferred_element_type=jnp.float32
            )
        acc[0, kb] += jnp.dot(qt[i], wide[1], preferred_element_type=jnp.float32)
        acc[1, kb] += jnp.dot(gt[i], wide[0], preferred_element_type=jnp.float32)

    def back_slot(slot, _):
        @pl.when(block - (distance - slot) >= 0)
        def _():
            def key_step(t, _):
                kb = slot * per_block + t

                def row_step(i, _):
                    back_tile(slot, t, i)
                    return 0

                lax.fori_loop(0, jnp.minimum(kb + 1, per_block), row_step, 0)
                send_term(slot, t)
                return 0

            lax.fori_loop(0, per_block, key_step, 0)

        return 0

    strides = min(per_block, 2)
    near = distance - 1

    def back_rows(first, _):
        @pl.when(has_prev)
        def _():
            def key_step(t, _):
                def row_step(j, _):
                    i = j * strides + first

                    @pl.when(i <= near * per_block + t)
                    def _():
                        back_tile(near, t, i)

                    return 0

                lax.fori_loop(0, per_block // strides, row_step, 0)

                @pl.when(first == strides - 1)
                def _():
                    send_term(near, t)

                return 0

            lax.fori_loop(0, per_block, key_step, 0)

        def own_rows(j, _):
            i = (per_block // strides - 1 - j) * strides + first

            def own_step(t, _):
                back_tile(distance, t, i)
                return 0

            lax.fori_loop(0, i + 1, own_step, 0)
            for h in range(share):
                dq[tile_rows(i), cols[h]] = (dqs[i, spans[h], :] * scale).astype(jnp.bfloat16)
            tile_out(out_at + 1, i, dq, q_cols, do_ref)
            return 0

        lax.fori_loop(0, per_block // strides, own_rows, 0)
        return 0

    def close_term(slot, c, t):
        by = scale if c == 0 else 1.0
        term = (acc[c, slot * per_block + t] * by).T

        @pl.when((slot > 0) & has_next)
        def _():
            hop_out(slot - 1, c, t).wait_recv()
            both = term + landed[slot - 1, c, tile_rows(t), :].astype(jnp.float32)
            sums[slot, c, tile_rows(t), :] = both.astype(jnp.bfloat16)

        @pl.when(jnp.logical_not((slot > 0) & has_next))
        def _():
            sums[slot, c, tile_rows(t), :] = term.astype(jnp.bfloat16)

    def send_term(slot, t):
        for c in range(2):
            close_term(slot, c, t)
        for c in range(2):
            hop_out(slot, c, t).start()

    lax.fori_loop(0, distance - 1, back_slot, 0)
    lax.fori_loop(0, strides, back_rows, 0)

    def finish(t, _):
        for c in range(2):
            close_term(distance, c, t)
        tile_out(out_at + 2, t, sums.at[distance, 0], HD, ko_ref)
        tile_out(out_at + 3, t, sums.at[distance, 1], HD, vo_ref)
        return 0

    lax.fori_loop(0, per_block, finish, 0)
    for pair in kv_swap + q_swap + g_swap:
        for copy in pair[1]:
            copy.wait_send()
    end_out(out_at, att, q_cols, ao_ref)
    end_out(out_at + 1, dq, q_cols, do_ref)
    end_out(out_at + 2, sums.at[distance, 0], HD, ko_ref)
    end_out(out_at + 3, sums.at[distance, 1], HD, vo_ref)
    for c in range(2):
        for step in range(distance):
            @pl.when((block - step >= 0) & has_next)
            def _():
                hop_in(step, c).wait_send()

            @pl.when(block - (distance - step) >= 0)
            def _():
                for t in range(per_block):
                    hop_out(step, c, t).wait_send()


def pass_kernel(*refs):
    ins, outs, held, (in_sem, out_sem) = refs[:4], refs[4:8], refs[8:12], refs[12:]
    loads = [pltpu.make_async_copy(ins[n], held[n], in_sem.at[n]) for n in range(4)]
    stores = [pltpu.make_async_copy(held[n], outs[n], out_sem.at[n]) for n in range(4)]
    for load in loads:
        load.start()
    for load, store in zip(loads, stores):
        load.wait()
        store.start()
    for store in stores:
        store.wait()


def per_device(queries, keys, values, grad_out, doc_ids):
    heads = lax.axis_size("head")
    peers = lax.axis_size("ctx")
    rows = queries.shape[0]
    group = keys.shape[1] // HD
    share = queries.shape[1] // HD // group
    ctx_low = group // heads
    blocks = peers // ctx_low
    tokens = rows * group
    distance = DOC_MOST // tokens
    bf16, f32 = jnp.bfloat16, jnp.float32
    vmem = pl.BlockSpec(memory_space=pltpu.VMEM)
    hbm = pl.BlockSpec(memory_space=pl.ANY)
    dma = pltpu.SemaphoreType.DMA
    tiles = tokens // TILE
    span = share * TILE
    all_tiles = (distance + 1) * tiles
    swaps = 2 + 2 * share + 4
    outs = pl.pallas_call(
        functools.partial(fused_kernel, heads, ctx_low, blocks, distance, HD ** -0.5),
        out_shape=(
            jax.ShapeDtypeStruct(queries.shape, bf16),
            jax.ShapeDtypeStruct(queries.shape, bf16),
            jax.ShapeDtypeStruct(keys.shape, bf16),
            jax.ShapeDtypeStruct(keys.shape, bf16),
        ),
        in_specs=[vmem] + [hbm] * 4,
        out_specs=(hbm,) * 4,
        scratch_shapes=[
            pltpu.VMEM((tiles, span, HD), bf16),
            pltpu.VMEM((tiles, span, HD), bf16),
            pltpu.VMEM((distance + 1, 2, tokens, HD), bf16),
            pltpu.VMEM((2, all_tiles, HD, TILE), f32),
            pltpu.VMEM((tiles, distance * tiles + 1, span, TILE), f32),
            pltpu.VMEM((tiles, span, HD), f32),
            pltpu.VMEM((span, HD), f32),
            pltpu.VMEM((span, HD), f32),
            pltpu.VMEM((tiles, span, HD), f32),
            pltpu.VMEM((tiles, HD, span), bf16),
            pltpu.VMEM((tiles, HD, span), bf16),
            pltpu.VMEM((tiles, span, HD), f32),
            pltpu.VMEM((tiles, span, HD), f32),
            pltpu.VMEM((tokens, share * HD), bf16),
            pltpu.VMEM((tokens, share * HD), bf16),
            pltpu.VMEM((distance + 1, 2, tokens, HD), bf16),
            pltpu.VMEM((distance, 2, tokens, HD), bf16),
            pltpu.VMEM((2, span, TILE), bf16),
            pltpu.VMEM((tiles, TILE, HD), jnp.int32),
            dma((swaps,)), dma((swaps, group - 1)), dma((swaps, group - 1)),
            dma((distance, 2)), dma((distance, 2)),
            dma((distance, 2, tiles)), dma((distance, 2, tiles)),
        ],
        compiler_params=pltpu.CompilerParams(
            collective_id=1, has_side_effects=True, vmem_limit_bytes=67043328
        ),
        name="fused",
    )(doc_ids.reshape(-1, 1, TILE), queries, keys, values, grad_out)
    return pl.pallas_call(
        pass_kernel,
        out_shape=tuple(jax.ShapeDtypeStruct(o.shape, o.dtype) for o in outs),
        in_specs=[hbm] * 4,
        out_specs=(hbm,) * 4,
        scratch_shapes=[pltpu.VMEM(o.shape, o.dtype) for o in outs] + [dma((4,)), dma((4,))],
        name="hand_on",
    )(*outs)


def solution(mesh):
    spec = P(("ctx", "head"), None)
    return jax.shard_map(
        per_device,
        mesh=mesh,
        in_specs=(spec, spec, spec, spec, P()),
        out_specs=(spec, spec, spec, spec),
        check_vma=False,
    )
```

```python
import functools

import jax
import jax.numpy as jnp
from jax import lax
from jax.experimental import pallas as pl
from jax.experimental.pallas import tpu as pltpu
from jax.sharding import PartitionSpec as P

HD = 128
DOC_MOST = 2048
TILE = 256
LOG2E = 1.4426950408889634
MESH = pl.DeviceIdType.MESH


def place(ctx_low, heads):
    ctx, head = lax.axis_index("ctx"), lax.axis_index("head")
    block = ctx // ctx_low
    me = (ctx - block * ctx_low) * heads + head

    def member(number):
        return (block * ctx_low + number // heads, lax.rem(number, heads))

    return ctx, head, block, me, member


def greet(members, ctx, head, ctx_low, has_prev, has_next):
    barrier = pltpu.get_barrier_semaphore()
    for device in members:
        pl.semaphore_signal(barrier, inc=1, device_id=device, device_id_type=MESH)

    @pl.when(has_prev)
    def _():
        pl.semaphore_signal(barrier, inc=1, device_id=(ctx - ctx_low, head), device_id_type=MESH)

    @pl.when(has_next)
    def _():
        pl.semaphore_signal(barrier, inc=1, device_id=(ctx + ctx_low, head), device_id_type=MESH)

    near = has_prev.astype(jnp.int32) + has_next.astype(jnp.int32)
    pl.semaphore_wait(barrier, len(members) + near)


def fused_kernel(
    heads, ctx_low, blocks, distance, scale,
    doc_ref, q_in, k_in, v_in, g_in,
    ao_ref, do_ref, ko_ref, vo_ref,
    qo, go, band, acc, kept, peak, total, made, dqs, qt, gt, inv, delta,
    att, dq, sums, landed, wide, row_doc,
    own_sem, send_sem, recv_sem, in_send, in_recv, out_send, out_recv,
):
    group = ctx_low * heads
    rows = q_in.shape[0]
    q_cols = q_in.shape[1] // group
    tokens = qo.shape[0] * TILE
    share = q_cols // HD
    factor = scale * LOG2E
    per_block = tokens // TILE
    per_tile = TILE // rows
    reach = distance * per_block + 1
    ctx, head, block, me, member = place(ctx_low, heads)
    has_prev, has_next = block > 0, block < blocks - 1
    others = [lax.rem(me + step, group) for step in range(1, group)]
    greet([member(o) for o in others], ctx, head, ctx_low, has_prev, has_next)
    my_tile = me // per_tile
    my_row = (me - my_tile * per_tile) * rows
    mine = pl.ds(pl.multiple_of(me * rows, rows), rows)
    first_tile = (block - distance) * per_block
    first_kb = jnp.maximum(distance - block, 0) * per_block

    def columns(width, number):
        return pl.ds(pl.multiple_of(number * width, width), width)

    def swap_in(a, src, first, width, dst):
        def part(number):
            return src.at[:, pl.ds(pl.multiple_of(number * width + first, HD), HD)]

        local = pltpu.make_async_copy(part(me), dst, own_sem.at[a])
        local.start()
        line = []
        for step, other in enumerate(others):
            copy = pltpu.make_async_remote_copy(
                src_ref=part(other), dst_ref=dst,
                send_sem=send_sem.at[a, step], recv_sem=recv_sem.at[a, step],
                device_id=member(other), device_id_type=MESH,
            )
            copy.start()
            line.append(copy)
        return local, line

    def head_rows(h):
        return pl.ds(pl.multiple_of(h * TILE + my_row, rows), rows)

    def settle(pair):
        pair[0].wait()
        for copy in pair[1]:
            copy.wait_recv()

    def tile_out(a, i, src, width, dst):
        def one(j, _):
            number = i * per_tile + j
            step = lax.rem(number - me + group, group)
            piece = src.at[pl.ds(pl.multiple_of(number * rows, rows), rows)]
            place_there = dst.at[:, columns(width, me)]

            @pl.when(step == 0)
            def _():
                pltpu.make_async_copy(piece, place_there, own_sem.at[a]).start()

            @pl.when(step > 0)
            def _():
                pltpu.make_async_remote_copy(
                    src_ref=piece, dst_ref=place_there,
                    send_sem=send_sem.at[a, step - 1], recv_sem=recv_sem.at[a, step - 1],
                    device_id=member(number), device_id_type=MESH,
                ).start()

            return 0

        lax.fori_loop(0, per_tile, one, 0)

    def end_out(a, src, width, dst):
        piece, place_there = src.at[mine], dst.at[:, columns(width, me)]
        pltpu.make_async_copy(piece, place_there, own_sem.at[a]).wait()
        for step, other in enumerate(others):
            copy = pltpu.make_async_remote_copy(
                src_ref=src.at[pl.ds(pl.multiple_of(other * rows, rows), rows)],
                dst_ref=place_there,
                send_sem=send_sem.at[a, step], recv_sem=recv_sem.at[a, step],
                device_id=member(other), device_id_type=MESH,
            )
            copy.wait_recv()
            copy.wait_send()

    def hop_in(step, c):
        return pltpu.make_async_remote_copy(
            src_ref=band.at[distance - step, c], dst_ref=band.at[distance - step - 1, c],
            send_sem=in_send.at[step, c], recv_sem=in_recv.at[step, c],
            device_id=(ctx + ctx_low, head), device_id_type=MESH,
        )

    def hop_out(step, c, t):
        return pltpu.make_async_remote_copy(
            src_ref=sums.at[step, c, tile_rows(t)], dst_ref=landed.at[step, c, tile_rows(t)],
            send_sem=out_send.at[step, c, t], recv_sem=out_recv.at[step, c, t],
            device_id=(ctx - ctx_low, head), device_id_type=MESH,
        )

    def tile_rows(i):
        return pl.ds(pl.multiple_of(i * TILE, TILE), TILE)

    kv_swap = [
        swap_in(0, k_in, 0, HD, band.at[distance, 0, mine]),
        swap_in(1, v_in, 0, HD, band.at[distance, 1, mine]),
    ]
    q_swap = [
        swap_in(2 + h, q_in, h * HD, q_cols, qo.at[my_tile, head_rows(h)]) for h in range(share)
    ]
    out_at = 2 + 2 * share
    acc[...] = jnp.zeros_like(acc)
    dqs[...] = jnp.zeros_like(dqs)
    peak[...] = jnp.full_like(peak, -1e30)
    for i in range(per_block):
        row_doc[i] = jnp.broadcast_to(doc_ref[block * per_block + i], (HD, TILE)).T
    for c in range(2):
        settle(kv_swap[c])

        @pl.when(has_next)
        def _():
            hop_in(0, c).start()

    for step in range(1, distance):
        @pl.when(block - step >= 0)
        def _():
            for c in range(2):
                hop_in(step - 1, c).wait_recv()

                @pl.when(has_next)
                def _():
                    hop_in(step, c).start()

    for pair in q_swap:
        settle(pair)
    g_swap = [
        swap_in(2 + share + h, g_in, h * HD, q_cols, go.at[my_tile, head_rows(h)])
        for h in range(share)
    ]

    spans = [slice(h * TILE, (h + 1) * TILE) for h in range(share)]
    cols = [slice(h * HD, (h + 1) * HD) for h in range(share)]

    def across(x, y):
        return lax.dot_general(
            x, y, (((1,), (1,)), ((), ())), preferred_element_type=jnp.float32
        )

    def twice(x):
        return jnp.concatenate([x, x], 1)

    def score_slot(n, _):
        slot = distance - n

        @pl.when(block - n >= 0)
        def _():
            @pl.when(n == distance)
            def _():
                hop_in(distance - 1, 0).wait_recv()

            def key_step(t, _):
                kb = slot * per_block + t

                def row_step(i, _):
                    keys = band[slot, 0, tile_rows(t), :]
                    away = lax.broadcasted_iota(jnp.int32, (TILE, TILE), 0) - (
                        lax.broadcasted_iota(jnp.int32, (TILE, TILE), 1)
                    )
                    same = twice(row_doc[i]) == doc_ref[first_tile + kb]
                    seen = same & (away >= (kb - i - reach + 1) * TILE)
                    for h in range(share):
                        s = jnp.where(seen, across(qo[i, spans[h], :], keys), -1e30)
                        kept[i, kb - i, spans[h], :] = s
                        both = jnp.maximum(s[:, :HD], s[:, HD:])
                        peak[i, spans[h], :] = jnp.maximum(peak[i, spans[h], :], both)
                    return 0

                lax.fori_loop(
                    jnp.maximum(kb - reach + 1, 0), jnp.minimum(kb + 1, per_block), row_step, 0
                )
                return 0

            lax.fori_loop(0, per_block, key_step, 0)

        return 0

    lax.fori_loop(0, distance + 1, score_slot, 0)

    @pl.when(block - distance >= 0)
    def _():
        hop_in(distance - 1, 1).wait_recv()

    def forward_tile(i, _):
        here = tile_rows(i)
        for h in range(share):
            top = jnp.max(peak[i, spans[h], :], 1, keepdims=True) * factor
            peak[i, spans[h], :] = jnp.broadcast_to(top, (TILE, HD))
        total[...] = jnp.zeros_like(total)
        made[...] = jnp.zeros_like(made)

        def forward(kb, _):
            slot = kb // per_block
            values = band[slot, 1, tile_rows(kb - slot * per_block), :]
            for h in range(share):
                span = spans[h]
                p = jnp.exp2(kept[i, kb - i, span, :] * factor - twice(peak[i, span, :]))
                kept[i, kb - i, span, :] = p
                total[span, :] += p[:, :HD] + p[:, HD:]
                made[span, :] += jnp.dot(
                    p.astype(jnp.bfloat16), values, preferred_element_type=jnp.float32
                )
            return 0

        lax.fori_loop(jnp.maximum(i, first_kb), i + reach, forward, 0)
        for h in range(share):
            span = spans[h]
            inverse = 1.0 / jnp.sum(total[span, :], 1, keepdims=True)
            inv[i, span, :] = jnp.broadcast_to(inverse, (TILE, HD))
            out = made[span, :] * inverse
            delta[i, span, :] = out
            att[here, cols[h]] = out.astype(jnp.bfloat16)
            qt[i, :, span] = qo[i, span, :].T
        tile_out(out_at, i, att, q_cols, ao_ref)
        return 0

    lax.fori_loop(0, per_block, forward_tile, 0)

    for pair in g_swap:
        settle(pair)

    def shift_tile(i, _):
        for h in range(share):
            span = spans[h]
            grads = go[i, span, :].astype(jnp.float32)
            shift = jnp.sum(delta[i, span, :] * grads, 1, keepdims=True)
            shares = inv[i, span, :]
            delta[i, span, :] = shift * shares
            grads = (grads * shares).astype(jnp.bfloat16)
            go[i, span, :] = grads
            gt[i, :, span] = grads.T
        return 0

    lax.fori_loop(0, per_block, shift_tile, 0)

    def back_both(slot, t, one, two):
        kb = slot * per_block + t
        keys = band[slot, 0, tile_rows(t), :]
        values = band[slot, 1, tile_rows(t), :]
        for n, i in enumerate((one, two)):
            for h in range(share):
                span = spans[h]
                w = kept[i, kb - i, span, :]
                dp = across(go[i, span, :], values)
                wide[2 * n, span, :] = w.astype(jnp.bfloat16)
                grown = w * (dp - twice(delta[i, span, :]))
                wide[2 * n + 1, span, :] = grown.astype(jnp.bfloat16)
        for n, i in enumerate((one, two)):
            for h in range(share):
                dqs[i, spans[h], :] += jnp.dot(
                    wide[2 * n + 1, spans[h], :], keys, preferred_element_type=jnp.float32
                )
        acc[0, kb] += jnp.dot(qt[one], wide[1], preferred_element_type=jnp.float32) + jnp.dot(
            qt[two], wide[3], preferred_element_type=jnp.float32
        )
        acc[1, kb] += jnp.dot(gt[one], wide[0], preferred_element_type=jnp.float32) + jnp.dot(
            gt[two], wide[2], preferred_element_type=jnp.float32
        )

    def back_tile(slot, t, i):
        kb = slot * per_block + t
        keys = band[slot, 0, tile_rows(t), :]
        values = band[slot, 1, tile_rows(t), :]
        for h in range(share):
            span = spans[h]
            w = kept[i, kb - i, span, :]
            dp = across(go[i, span, :], values)
            wide[0, span, :] = w.astype(jnp.bfloat16)
            wide[1, span, :] = (w * (dp - twice(delta[i, span, :]))).astype(jnp.bfloat16)
        for h in range(share):
            dqs[i, spans[h], :] += jnp.dot(
                wide[1, spans[h], :], keys, preferred_element_type=jnp.float32
            )
        acc[0, kb] += jnp.dot(qt[i], wide[1], preferred_element_type=jnp.float32)
        acc[1, kb] += jnp.dot(gt[i], wide[0], preferred_element_type=jnp.float32)

    def back_slot(slot, _):
        @pl.when(block - (distance - slot) >= 0)
        def _():
            def key_step(t, _):
                kb = slot * per_block + t

                count = jnp.minimum(kb + 1, per_block)

                def row_step(j, _):
                    back_both(slot, t, 2 * j, 2 * j + 1)
                    return 0

                if per_block > 1:
                    lax.fori_loop(0, count // 2, row_step, 0)

                @pl.when(lax.rem(count, 2) == 1)
                def _():
                    back_tile(slot, t, count - 1)

                send_term(slot, t)
                return 0

            lax.fori_loop(0, per_block, key_step, 0)

        return 0

    strides = min(per_block, 2)
    near = distance - 1

    def back_rows(first, _):
        @pl.when(has_prev)
        def _():
            def key_step(t, _):
                kb = near * per_block + t
                if strides * 2 == per_block:
                    @pl.when(strides + first <= kb)
                    def _():
                        back_both(near, t, first, strides + first)

                    @pl.when((first <= kb) & (strides + first > kb))
                    def _():
                        back_tile(near, t, first)
                else:
                    def row_step(j, _):
                        @pl.when(j * strides + first <= kb)
                        def _():
                            back_tile(near, t, j * strides + first)

                        return 0

                    lax.fori_loop(0, per_block // strides, row_step, 0)

                @pl.when(first == strides - 1)
                def _():
                    send_term(near, t)

                return 0

            lax.fori_loop(0, per_block, key_step, 0)

        def own_step(t, _):
            if strides * 2 == per_block:
                @pl.when(t <= first)
                def _():
                    back_both(distance, t, first, strides + first)

                @pl.when((t > first) & (t <= strides + first))
                def _():
                    back_tile(distance, t, strides + first)
            else:
                def row_step(j, _):
                    @pl.when(t <= j * strides + first)
                    def _():
                        back_tile(distance, t, j * strides + first)

                    return 0

                lax.fori_loop(0, per_block // strides, row_step, 0)

            @pl.when(lax.rem(t, strides) == first)
            def _():
                for h in range(share):
                    grown = dqs[t, spans[h], :] * scale
                    dq[tile_rows(t), cols[h]] = grown.astype(jnp.bfloat16)
                tile_out(out_at + 1, t, dq, q_cols, do_ref)

            return 0

        lax.fori_loop(0, per_block, own_step, 0)
        return 0

    def close_term(slot, c, t):
        by = scale if c == 0 else 1.0
        term = (acc[c, slot * per_block + t] * by).T

        @pl.when((slot > 0) & has_next)
        def _():
            hop_out(slot - 1, c, t).wait_recv()
            both = term + landed[slot - 1, c, tile_rows(t), :].astype(jnp.float32)
            sums[slot, c, tile_rows(t), :] = both.astype(jnp.bfloat16)

        @pl.when(jnp.logical_not((slot > 0) & has_next))
        def _():
            sums[slot, c, tile_rows(t), :] = term.astype(jnp.bfloat16)

    def send_term(slot, t):
        for c in range(2):
            close_term(slot, c, t)
        for c in range(2):
            hop_out(slot, c, t).start()

    lax.fori_loop(0, distance - 1, back_slot, 0)
    lax.fori_loop(0, strides, back_rows, 0)

    def finish(t, _):
        for c in range(2):
            close_term(distance, c, t)
        tile_out(out_at + 2, t, sums.at[distance, 0], HD, ko_ref)
        tile_out(out_at + 3, t, sums.at[distance, 1], HD, vo_ref)
        return 0

    lax.fori_loop(0, per_block, finish, 0)
    for pair in kv_swap + q_swap + g_swap:
        for copy in pair[1]:
            copy.wait_send()
    end_out(out_at, att, q_cols, ao_ref)
    end_out(out_at + 1, dq, q_cols, do_ref)
    end_out(out_at + 2, sums.at[distance, 0], HD, ko_ref)
    end_out(out_at + 3, sums.at[distance, 1], HD, vo_ref)
    for c in range(2):
        for step in range(distance):
            @pl.when((block - step >= 0) & has_next)
            def _():
                hop_in(step, c).wait_send()

            @pl.when(block - (distance - step) >= 0)
            def _():
                for t in range(per_block):
                    hop_out(step, c, t).wait_send()


def pass_kernel(*refs):
    ins, outs, held, (in_sem, out_sem) = refs[:4], refs[4:8], refs[8:12], refs[12:]
    loads = [pltpu.make_async_copy(ins[n], held[n], in_sem.at[n]) for n in range(4)]
    stores = [pltpu.make_async_copy(held[n], outs[n], out_sem.at[n]) for n in range(4)]
    for load in loads:
        load.start()
    for load, store in zip(loads, stores):
        load.wait()
        store.start()
    for store in stores:
        store.wait()


def per_device(queries, keys, values, grad_out, doc_ids):
    heads = lax.axis_size("head")
    peers = lax.axis_size("ctx")
    rows = queries.shape[0]
    group = keys.shape[1] // HD
    share = queries.shape[1] // HD // group
    ctx_low = group // heads
    blocks = peers // ctx_low
    tokens = rows * group
    distance = DOC_MOST // tokens
    bf16, f32 = jnp.bfloat16, jnp.float32
    vmem = pl.BlockSpec(memory_space=pltpu.VMEM)
    hbm = pl.BlockSpec(memory_space=pl.ANY)
    dma = pltpu.SemaphoreType.DMA
    tiles = tokens // TILE
    span = share * TILE
    all_tiles = (distance + 1) * tiles
    swaps = 2 + 2 * share + 4
    outs = pl.pallas_call(
        functools.partial(fused_kernel, heads, ctx_low, blocks, distance, HD ** -0.5),
        out_shape=(
            jax.ShapeDtypeStruct(queries.shape, bf16),
            jax.ShapeDtypeStruct(queries.shape, bf16),
            jax.ShapeDtypeStruct(keys.shape, bf16),
            jax.ShapeDtypeStruct(keys.shape, bf16),
        ),
        in_specs=[vmem] + [hbm] * 4,
        out_specs=(hbm,) * 4,
        scratch_shapes=[
            pltpu.VMEM((tiles, span, HD), bf16),
            pltpu.VMEM((tiles, span, HD), bf16),
            pltpu.VMEM((distance + 1, 2, tokens, HD), bf16),
            pltpu.VMEM((2, all_tiles, HD, TILE), f32),
            pltpu.VMEM((tiles, distance * tiles + 1, span, TILE), f32),
            pltpu.VMEM((tiles, span, HD), f32),
            pltpu.VMEM((span, HD), f32),
            pltpu.VMEM((span, HD), f32),
            pltpu.VMEM((tiles, span, HD), f32),
            pltpu.VMEM((tiles, HD, span), bf16),
            pltpu.VMEM((tiles, HD, span), bf16),
            pltpu.VMEM((tiles, span, HD), f32),
            pltpu.VMEM((tiles, span, HD), f32),
            pltpu.VMEM((tokens, share * HD), bf16),
            pltpu.VMEM((tokens, share * HD), bf16),
            pltpu.VMEM((distance + 1, 2, tokens, HD), bf16),
            pltpu.VMEM((distance, 2, tokens, HD), bf16),
            pltpu.VMEM((4, span, TILE), bf16),
            pltpu.VMEM((tiles, TILE, HD), jnp.int32),
            dma((swaps,)), dma((swaps, group - 1)), dma((swaps, group - 1)),
            dma((distance, 2)), dma((distance, 2)),
            dma((distance, 2, tiles)), dma((distance, 2, tiles)),
        ],
        compiler_params=pltpu.CompilerParams(
            collective_id=1, has_side_effects=True, vmem_limit_bytes=67043328
        ),
        name="fused",
    )(doc_ids.reshape(-1, 1, TILE), queries, keys, values, grad_out)
    return pl.pallas_call(
        pass_kernel,
        out_shape=tuple(jax.ShapeDtypeStruct(o.shape, o.dtype) for o in outs),
        in_specs=[hbm] * 4,
        out_specs=(hbm,) * 4,
        scratch_shapes=[pltpu.VMEM(o.shape, o.dtype) for o in outs] + [dma((4,)), dma((4,))],
        name="hand_on",
    )(*outs)


def solution(mesh):
    spec = P(("ctx", "head"), None)
    return jax.shard_map(
        per_device,
        mesh=mesh,
        in_specs=(spec, spec, spec, spec, P()),
        out_specs=(spec, spec, spec, spec),
        check_vma=False,
    )
```

```python
import functools

import jax
import jax.numpy as jnp
from jax import lax
from jax.experimental import pallas as pl
from jax.experimental.pallas import tpu as pltpu
from jax.sharding import PartitionSpec as P

HD = 128
DOC_MOST = 2048
TILE = 256
LOG2E = 1.4426950408889634
MESH = pl.DeviceIdType.MESH


def place(ctx_low, heads):
    ctx, head = lax.axis_index("ctx"), lax.axis_index("head")
    block = ctx // ctx_low
    me = (ctx - block * ctx_low) * heads + head

    def member(number):
        return (block * ctx_low + number // heads, lax.rem(number, heads))

    return ctx, head, block, me, member


def greet(members, ctx, head, ctx_low, has_prev, has_next):
    barrier = pltpu.get_barrier_semaphore()
    for device in members:
        pl.semaphore_signal(barrier, inc=1, device_id=device, device_id_type=MESH)

    @pl.when(has_prev)
    def _():
        pl.semaphore_signal(barrier, inc=1, device_id=(ctx - ctx_low, head), device_id_type=MESH)

    @pl.when(has_next)
    def _():
        pl.semaphore_signal(barrier, inc=1, device_id=(ctx + ctx_low, head), device_id_type=MESH)

    near = has_prev.astype(jnp.int32) + has_next.astype(jnp.int32)
    pl.semaphore_wait(barrier, len(members) + near)


def fused_kernel(
    heads, ctx_low, blocks, distance, scale,
    doc_ref, q_in, k_in, v_in, g_in,
    ao_ref, do_ref, ko_ref, vo_ref,
    qo, go, band, acc, kept, peak, total, made, dqs, qt, gt, inv, delta,
    att, dq, sums, landed, wide, row_doc,
    own_sem, send_sem, recv_sem, in_send, in_recv, out_send, out_recv,
):
    group = ctx_low * heads
    rows = q_in.shape[0]
    q_cols = q_in.shape[1] // group
    tokens = qo.shape[0] * TILE
    share = q_cols // HD
    factor = scale * LOG2E
    per_block = tokens // TILE
    per_tile = TILE // rows
    reach = distance * per_block + 1
    ctx, head, block, me, member = place(ctx_low, heads)
    has_prev, has_next = block > 0, block < blocks - 1
    others = [lax.rem(me + step, group) for step in range(1, group)]
    greet([member(o) for o in others], ctx, head, ctx_low, has_prev, has_next)
    my_tile = me // per_tile
    my_row = (me - my_tile * per_tile) * rows
    mine = pl.ds(pl.multiple_of(me * rows, rows), rows)
    first_tile = (block - distance) * per_block
    first_kb = jnp.maximum(distance - block, 0) * per_block

    def columns(width, number):
        return pl.ds(pl.multiple_of(number * width, width), width)

    def swap_in(a, src, first, width, dst):
        def part(number):
            return src.at[:, pl.ds(pl.multiple_of(number * width + first, HD), HD)]

        local = pltpu.make_async_copy(part(me), dst, own_sem.at[a])
        local.start()
        line = []
        for step, other in enumerate(others):
            copy = pltpu.make_async_remote_copy(
                src_ref=part(other), dst_ref=dst,
                send_sem=send_sem.at[a, step], recv_sem=recv_sem.at[a, step],
                device_id=member(other), device_id_type=MESH,
            )
            copy.start()
            line.append(copy)
        return local, line

    def head_rows(h):
        return pl.ds(pl.multiple_of(h * TILE + my_row, rows), rows)

    def settle(pair):
        pair[0].wait()
        for copy in pair[1]:
            copy.wait_recv()

    def tile_out(a, i, src, width, dst):
        def one(j, _):
            number = i * per_tile + j
            step = lax.rem(number - me + group, group)
            piece = src.at[pl.ds(pl.multiple_of(number * rows, rows), rows)]
            place_there = dst.at[:, columns(width, me)]

            @pl.when(step == 0)
            def _():
                pltpu.make_async_copy(piece, place_there, own_sem.at[a]).start()

            @pl.when(step > 0)
            def _():
                pltpu.make_async_remote_copy(
                    src_ref=piece, dst_ref=place_there,
                    send_sem=send_sem.at[a, step - 1], recv_sem=recv_sem.at[a, step - 1],
                    device_id=member(number), device_id_type=MESH,
                ).start()

            return 0

        lax.fori_loop(0, per_tile, one, 0)

    def end_out(a, src, width, dst):
        piece, place_there = src.at[mine], dst.at[:, columns(width, me)]
        pltpu.make_async_copy(piece, place_there, own_sem.at[a]).wait()
        for step, other in enumerate(others):
            copy = pltpu.make_async_remote_copy(
                src_ref=src.at[pl.ds(pl.multiple_of(other * rows, rows), rows)],
                dst_ref=place_there,
                send_sem=send_sem.at[a, step], recv_sem=recv_sem.at[a, step],
                device_id=member(other), device_id_type=MESH,
            )
            copy.wait_recv()
            copy.wait_send()

    def hop_in(step, c):
        return pltpu.make_async_remote_copy(
            src_ref=band.at[distance - step, c], dst_ref=band.at[distance - step - 1, c],
            send_sem=in_send.at[step, c], recv_sem=in_recv.at[step, c],
            device_id=(ctx + ctx_low, head), device_id_type=MESH,
        )

    def hop_out(step, c, t):
        return pltpu.make_async_remote_copy(
            src_ref=sums.at[step, c, tile_rows(t)], dst_ref=landed.at[step, c, tile_rows(t)],
            send_sem=out_send.at[step, c, t], recv_sem=out_recv.at[step, c, t],
            device_id=(ctx - ctx_low, head), device_id_type=MESH,
        )

    def tile_rows(i):
        return pl.ds(pl.multiple_of(i * TILE, TILE), TILE)

    kv_swap = [
        swap_in(0, k_in, 0, HD, band.at[distance, 0, mine]),
        swap_in(1, v_in, 0, HD, band.at[distance, 1, mine]),
    ]
    q_swap = [
        swap_in(2 + h, q_in, h * HD, q_cols, qo.at[my_tile, head_rows(h)]) for h in range(share)
    ]
    out_at = 2 + 2 * share
    acc[...] = jnp.zeros_like(acc)
    dqs[...] = jnp.zeros_like(dqs)
    peak[...] = jnp.full_like(peak, -1e30)
    for i in range(per_block):
        row_doc[i] = jnp.broadcast_to(doc_ref[block * per_block + i], (HD, TILE)).T
    for c in range(2):
        settle(kv_swap[c])

        @pl.when(has_next)
        def _():
            hop_in(0, c).start()

    for step in range(1, distance):
        @pl.when(block - step >= 0)
        def _():
            for c in range(2):
                hop_in(step - 1, c).wait_recv()

                @pl.when(has_next)
                def _():
                    hop_in(step, c).start()

    for pair in q_swap:
        settle(pair)
    g_swap = [
        swap_in(2 + share + h, g_in, h * HD, q_cols, go.at[my_tile, head_rows(h)])
        for h in range(share)
    ]

    spans = [slice(h * TILE, (h + 1) * TILE) for h in range(share)]
    cols = [slice(h * HD, (h + 1) * HD) for h in range(share)]

    def across(x, y):
        return lax.dot_general(
            x, y, (((1,), (1,)), ((), ())), preferred_element_type=jnp.float32
        )

    def twice(x):
        return jnp.concatenate([x, x], 1)

    def score_slot(n, _):
        slot = distance - n

        @pl.when(block - n >= 0)
        def _():
            @pl.when(n == distance)
            def _():
                hop_in(distance - 1, 0).wait_recv()

            def key_step(t, _):
                kb = slot * per_block + t

                def row_step(i, _):
                    keys = band[slot, 0, tile_rows(t), :]
                    away = lax.broadcasted_iota(jnp.int32, (TILE, TILE), 0) - (
                        lax.broadcasted_iota(jnp.int32, (TILE, TILE), 1)
                    )
                    same = twice(row_doc[i]) == doc_ref[first_tile + kb]
                    seen = same & (away >= (kb - i - reach + 1) * TILE)
                    for h in range(share):
                        s = jnp.where(seen, across(qo[i, spans[h], :], keys), -1e30)
                        kept[i, kb - i, spans[h], :] = s
                        both = jnp.maximum(s[:, :HD], s[:, HD:])
                        peak[i, spans[h], :] = jnp.maximum(peak[i, spans[h], :], both)
                    return 0

                lax.fori_loop(
                    jnp.maximum(kb - reach + 1, 0), jnp.minimum(kb + 1, per_block), row_step, 0
                )
                return 0

            lax.fori_loop(0, per_block, key_step, 0)

        return 0

    lax.fori_loop(0, distance + 1, score_slot, 0)

    @pl.when(block - distance >= 0)
    def _():
        hop_in(distance - 1, 1).wait_recv()

    def forward_tile(i, _):
        here = tile_rows(i)
        for h in range(share):
            top = jnp.max(peak[i, spans[h], :], 1, keepdims=True) * factor
            peak[i, spans[h], :] = jnp.broadcast_to(top, (TILE, HD))
        total[...] = jnp.zeros_like(total)
        made[...] = jnp.zeros_like(made)

        def part(kb, h):
            slot = kb // per_block
            values = band[slot, 1, tile_rows(kb - slot * per_block), :]
            span = spans[h]
            p = jnp.exp2(kept[i, kb - i, span, :] * factor - twice(peak[i, span, :]))
            kept[i, kb - i, span, :] = p
            grown = jnp.dot(p.astype(jnp.bfloat16), values, preferred_element_type=jnp.float32)
            return p[:, :HD] + p[:, HD:], grown

        def forward(n, _):
            kb = i + reach - 2 - 2 * n
            for h in range(share):
                sum_a, grown_a = part(kb, h)
                sum_b, grown_b = part(kb + 1, h)
                total[spans[h], :] += sum_a + sum_b
                made[spans[h], :] += grown_a + grown_b
            return 0

        lowest = jnp.maximum(i, first_kb)
        count = i + reach - lowest

        @pl.when(lax.rem(count, 2) == 1)
        def _():
            for h in range(share):
                sum_a, grown_a = part(lowest, h)
                total[spans[h], :] += sum_a
                made[spans[h], :] += grown_a

        lax.fori_loop(0, count // 2, forward, 0)
        for h in range(share):
            span = spans[h]
            inverse = 1.0 / jnp.sum(total[span, :], 1, keepdims=True)
            inv[i, span, :] = jnp.broadcast_to(inverse, (TILE, HD))
            out = made[span, :] * inverse
            delta[i, span, :] = out
            att[here, cols[h]] = out.astype(jnp.bfloat16)
            qt[i, :, span] = qo[i, span, :].T
        tile_out(out_at, i, att, q_cols, ao_ref)
        return 0

    lax.fori_loop(0, per_block, forward_tile, 0)

    for pair in g_swap:
        settle(pair)

    def shift_tile(i, _):
        for h in range(share):
            span = spans[h]
            grads = go[i, span, :].astype(jnp.float32)
            shift = jnp.sum(delta[i, span, :] * grads, 1, keepdims=True)
            shares = inv[i, span, :]
            delta[i, span, :] = shift * shares
            grads = (grads * shares).astype(jnp.bfloat16)
            go[i, span, :] = grads
            gt[i, :, span] = grads.T
        return 0

    lax.fori_loop(0, per_block, shift_tile, 0)

    def back_both(slot, t, one, two):
        kb = slot * per_block + t
        keys = band[slot, 0, tile_rows(t), :]
        values = band[slot, 1, tile_rows(t), :]
        for n, i in enumerate((one, two)):
            for h in range(share):
                span = spans[h]
                w = kept[i, kb - i, span, :]
                dp = across(go[i, span, :], values)
                wide[2 * n, span, :] = w.astype(jnp.bfloat16)
                grown = w * (dp - twice(delta[i, span, :]))
                wide[2 * n + 1, span, :] = grown.astype(jnp.bfloat16)
        for n, i in enumerate((one, two)):
            for h in range(share):
                dqs[i, spans[h], :] += jnp.dot(
                    wide[2 * n + 1, spans[h], :], keys, preferred_element_type=jnp.float32
                )
        acc[0, kb] += jnp.dot(qt[one], wide[1], preferred_element_type=jnp.float32) + jnp.dot(
            qt[two], wide[3], preferred_element_type=jnp.float32
        )
        acc[1, kb] += jnp.dot(gt[one], wide[0], preferred_element_type=jnp.float32) + jnp.dot(
            gt[two], wide[2], preferred_element_type=jnp.float32
        )

    def back_tile(slot, t, i):
        kb = slot * per_block + t
        keys = band[slot, 0, tile_rows(t), :]
        values = band[slot, 1, tile_rows(t), :]
        for h in range(share):
            span = spans[h]
            w = kept[i, kb - i, span, :]
            dp = across(go[i, span, :], values)
            wide[0, span, :] = w.astype(jnp.bfloat16)
            wide[1, span, :] = (w * (dp - twice(delta[i, span, :]))).astype(jnp.bfloat16)
        for h in range(share):
            dqs[i, spans[h], :] += jnp.dot(
                wide[1, spans[h], :], keys, preferred_element_type=jnp.float32
            )
        acc[0, kb] += jnp.dot(qt[i], wide[1], preferred_element_type=jnp.float32)
        acc[1, kb] += jnp.dot(gt[i], wide[0], preferred_element_type=jnp.float32)

    def back_slot(slot, _):
        @pl.when(block - (distance - slot) >= 0)
        def _():
            def key_step(t, _):
                kb = slot * per_block + t

                count = jnp.minimum(kb + 1, per_block)

                def row_step(j, _):
                    back_both(slot, t, 2 * j, 2 * j + 1)
                    return 0

                if per_block > 1:
                    lax.fori_loop(0, count // 2, row_step, 0)

                @pl.when(lax.rem(count, 2) == 1)
                def _():
                    back_tile(slot, t, count - 1)

                send_term(slot, t)
                return 0

            lax.fori_loop(0, per_block, key_step, 0)

        return 0

    strides = min(per_block, 2)
    near = distance - 1

    def back_rows(first, _):
        @pl.when(has_prev)
        def _():
            def key_step(t, _):
                kb = near * per_block + t
                if strides * 2 == per_block:
                    @pl.when(strides + first <= kb)
                    def _():
                        back_both(near, t, first, strides + first)

                    @pl.when((first <= kb) & (strides + first > kb))
                    def _():
                        back_tile(near, t, first)
                else:
                    def row_step(j, _):
                        @pl.when(j * strides + first <= kb)
                        def _():
                            back_tile(near, t, j * strides + first)

                        return 0

                    lax.fori_loop(0, per_block // strides, row_step, 0)

                @pl.when(first == strides - 1)
                def _():
                    send_term(near, t)

                return 0

            lax.fori_loop(0, per_block, key_step, 0)

        def own_step(t, _):
            if strides * 2 == per_block:
                @pl.when(t <= first)
                def _():
                    back_both(distance, t, first, strides + first)

                @pl.when((t > first) & (t <= strides + first))
                def _():
                    back_tile(distance, t, strides + first)
            else:
                def row_step(j, _):
                    @pl.when(t <= j * strides + first)
                    def _():
                        back_tile(distance, t, j * strides + first)

                    return 0

                lax.fori_loop(0, per_block // strides, row_step, 0)

            @pl.when(lax.rem(t, strides) == first)
            def _():
                for h in range(share):
                    grown = dqs[t, spans[h], :] * scale
                    dq[tile_rows(t), cols[h]] = grown.astype(jnp.bfloat16)
                tile_out(out_at + 1, t, dq, q_cols, do_ref)

            return 0

        lax.fori_loop(0, per_block, own_step, 0)
        return 0

    def close_term(slot, c, t):
        by = scale if c == 0 else 1.0
        term = (acc[c, slot * per_block + t] * by).T

        @pl.when((slot > 0) & has_next)
        def _():
            hop_out(slot - 1, c, t).wait_recv()
            both = term + landed[slot - 1, c, tile_rows(t), :].astype(jnp.float32)
            sums[slot, c, tile_rows(t), :] = both.astype(jnp.bfloat16)

        @pl.when(jnp.logical_not((slot > 0) & has_next))
        def _():
            sums[slot, c, tile_rows(t), :] = term.astype(jnp.bfloat16)

    def send_term(slot, t):
        for c in range(2):
            close_term(slot, c, t)
        for c in range(2):
            hop_out(slot, c, t).start()

    lax.fori_loop(0, distance - 1, back_slot, 0)
    lax.fori_loop(0, strides, back_rows, 0)

    def finish(t, _):
        for c in range(2):
            close_term(distance, c, t)
        tile_out(out_at + 2, t, sums.at[distance, 0], HD, ko_ref)
        tile_out(out_at + 3, t, sums.at[distance, 1], HD, vo_ref)
        return 0

    lax.fori_loop(0, per_block, finish, 0)
    for pair in kv_swap + q_swap + g_swap:
        for copy in pair[1]:
            copy.wait_send()
    end_out(out_at, att, q_cols, ao_ref)
    end_out(out_at + 1, dq, q_cols, do_ref)
    end_out(out_at + 2, sums.at[distance, 0], HD, ko_ref)
    end_out(out_at + 3, sums.at[distance, 1], HD, vo_ref)
    for c in range(2):
        for step in range(distance):
            @pl.when((block - step >= 0) & has_next)
            def _():
                hop_in(step, c).wait_send()

            @pl.when(block - (distance - step) >= 0)
            def _():
                for t in range(per_block):
                    hop_out(step, c, t).wait_send()


def pass_kernel(*refs):
    ins, outs, held, (in_sem, out_sem) = refs[:4], refs[4:8], refs[8:12], refs[12:]
    loads = [pltpu.make_async_copy(ins[n], held[n], in_sem.at[n]) for n in range(4)]
    stores = [pltpu.make_async_copy(held[n], outs[n], out_sem.at[n]) for n in range(4)]
    for load in loads:
        load.start()
    for load, store in zip(loads, stores):
        load.wait()
        store.start()
    for store in stores:
        store.wait()


def per_device(queries, keys, values, grad_out, doc_ids):
    heads = lax.axis_size("head")
    peers = lax.axis_size("ctx")
    rows = queries.shape[0]
    group = keys.shape[1] // HD
    share = queries.shape[1] // HD // group
    ctx_low = group // heads
    blocks = peers // ctx_low
    tokens = rows * group
    distance = DOC_MOST // tokens
    bf16, f32 = jnp.bfloat16, jnp.float32
    vmem = pl.BlockSpec(memory_space=pltpu.VMEM)
    hbm = pl.BlockSpec(memory_space=pl.ANY)
    dma = pltpu.SemaphoreType.DMA
    tiles = tokens // TILE
    span = share * TILE
    all_tiles = (distance + 1) * tiles
    swaps = 2 + 2 * share + 4
    outs = pl.pallas_call(
        functools.partial(fused_kernel, heads, ctx_low, blocks, distance, HD ** -0.5),
        out_shape=(
            jax.ShapeDtypeStruct(queries.shape, bf16),
            jax.ShapeDtypeStruct(queries.shape, bf16),
            jax.ShapeDtypeStruct(keys.shape, bf16),
            jax.ShapeDtypeStruct(keys.shape, bf16),
        ),
        in_specs=[vmem] + [hbm] * 4,
        out_specs=(hbm,) * 4,
        scratch_shapes=[
            pltpu.VMEM((tiles, span, HD), bf16),
            pltpu.VMEM((tiles, span, HD), bf16),
            pltpu.VMEM((distance + 1, 2, tokens, HD), bf16),
            pltpu.VMEM((2, all_tiles, HD, TILE), f32),
            pltpu.VMEM((tiles, distance * tiles + 1, span, TILE), f32),
            pltpu.VMEM((tiles, span, HD), f32),
            pltpu.VMEM((span, HD), f32),
            pltpu.VMEM((span, HD), f32),
            pltpu.VMEM((tiles, span, HD), f32),
            pltpu.VMEM((tiles, HD, span), bf16),
            pltpu.VMEM((tiles, HD, span), bf16),
            pltpu.VMEM((tiles, span, HD), f32),
            pltpu.VMEM((tiles, span, HD), f32),
            pltpu.VMEM((tokens, share * HD), bf16),
            pltpu.VMEM((tokens, share * HD), bf16),
            pltpu.VMEM((distance + 1, 2, tokens, HD), bf16),
            pltpu.VMEM((distance, 2, tokens, HD), bf16),
            pltpu.VMEM((4, span, TILE), bf16),
            pltpu.VMEM((tiles, TILE, HD), jnp.int32),
            dma((swaps,)), dma((swaps, group - 1)), dma((swaps, group - 1)),
            dma((distance, 2)), dma((distance, 2)),
            dma((distance, 2, tiles)), dma((distance, 2, tiles)),
        ],
        compiler_params=pltpu.CompilerParams(
            collective_id=1, has_side_effects=True, vmem_limit_bytes=67043328
        ),
        name="fused",
    )(doc_ids.reshape(-1, 1, TILE), queries, keys, values, grad_out)
    return pl.pallas_call(
        pass_kernel,
        out_shape=tuple(jax.ShapeDtypeStruct(o.shape, o.dtype) for o in outs),
        in_specs=[hbm] * 4,
        out_specs=(hbm,) * 4,
        scratch_shapes=[pltpu.VMEM(o.shape, o.dtype) for o in outs] + [dma((4,)), dma((4,))],
        name="hand_on",
    )(*outs)


def solution(mesh):
    spec = P(("ctx", "head"), None)
    return jax.shard_map(
        per_device,
        mesh=mesh,
        in_specs=(spec, spec, spec, spec, P()),
        out_specs=(spec, spec, spec, spec),
        check_vma=False,
    )
```
